256 devices in a mesh: sub: 64 (over z, y, core), grp: 4 (over x).
Axes of the slice: x: 4, y: 4, z: 8, core: 2. Of those that a mesh axis runs over, the one named last changes fastest.
Arguments:
- load_source: bfloat16 [4, 64, 32, 1536], P('grp', 'sub'), may hold values from -18 to 18
- schur_diag: float32 [4, 64, 1536], P('grp', 'sub'), may hold values from 0.3 to 3
- schur_factor: bfloat16 [4, 64, 1536, 1536], P('grp', 'sub'), may hold values from -0.15625 to 0.15625
- dir_diag: float32 [4, 64, 1536], P('grp', 'sub'), may hold values from 0.3 to 3
- dir_factor: bfloat16 [4, 64, 1536, 1536], P('grp', 'sub'), may hold values from -0.15625 to 0.15625
- corner_map: bfloat16 [4, 64, 24, 1536], P('grp', 'sub'), may hold values from -0.3125 to 0.3125
- corner_row: int32 [4, 64, 24], P('grp', 'sub'), may hold values from 0 to 2047
- coarse_factor: bfloat16 [2048, 2048], P(('sub', 'grp')), may hold values from -0.125 to 0.125
- slot_table: int32 [4, 64, 6, 256], P('grp', 'sub'), may hold values from 0 to 1536, as said below
Outputs:
- multipliers: float32 [4, 64, 32, 1536], P('grp', 'sub')
- residual: float32 [4, 64, 32, 1536], P('grp', 'sub')
The draws below stay inside these ranges and needn't reach their ends.
Inputs may be any that keep to these rules, and one draw needn't show every extreme that they name: slot_table[g, p, b, c] is the local slot of the c-th DOF that subdomain p shares with subdomain (p + k) mod 64 of group g, k = 1, 2, 5, -1, -2, -5 for b = 0 to 5; the neighbour lists the same DOF at the same c in its block (b + 3) mod 6; each pair shares 256 // 4 to 256 DOFs, listed first, and the rest of a block holds 1536; no slot appears twice in one subdomain; in every group some pair shares exactly 256.
All inputs are finite; a program needn't handle non-finite values.
Results may differ from the reference program's by a relative error of at most 0.01.
Values may be sent and summed in bfloat16 or wider, within the bound.
No kernel may reach another device: no remote copies, remote signals or barrier semaphores. Data moves between devices by JAX's collectives and lax.ppermute only.
A program may use at most 64 MiB of HBM per device.

```python
import math
import jax
import jax.numpy as jnp
from jax import lax

I = 1536
CASES = 32
NCR = 24
ITERS = 1
CAP = 256
SUBS = 64
GRPS = 4
NC = 2048


def draw_load_source(key, part):
    normal_key = jax.random.fold_in(jax.random.fold_in(key, 7), 0)
    position = jnp.arange(SUBS).astype(jnp.float32) / (SUBS - 1)
    rising = (3.0 ** position)[None, :, None, None]
    values = jax.random.normal(normal_key, (GRPS, SUBS, CASES, I), jnp.float32) * rising
    return jnp.clip(values, -18.0, 18.0).astype(jnp.bfloat16)


def draw_slot_table(key, part):
    count_key, order_key = jax.random.split(jax.random.fold_in(key, 11))
    shared = jax.random.randint(count_key, (GRPS, SUBS, 3), CAP // 4, CAP + 1)
    shared = shared.at[:, 0, 0].set(CAP)
    backward = jnp.stack([jnp.roll(shared[:, :, 0], 1, axis=1), jnp.roll(shared[:, :, 1], 2, axis=1), jnp.roll(shared[:, :, 2], 5, axis=1)], axis=2)
    counts = jnp.concatenate([shared, backward], axis=2)
    scores = jax.random.randint(order_key, (GRPS, SUBS, I), 0, 2 ** 20) * I + jnp.arange(I)[None, None, :]
    ordering = jnp.argsort(scores, axis=2).astype(jnp.int32)
    blocks = ordering.reshape(GRPS, SUBS, 6, CAP)
    column = jnp.arange(CAP)
    return jnp.where(column[None, None, None, :] < counts[:, :, :, None], blocks, I).astype(jnp.int32)


def place_ends(drawn, rng, smallest, top_value):
    place = [jax.random.randint(jax.random.fold_in(rng, axis), (), 0, length) for axis, length in enumerate(drawn.shape)]
    longest = drawn.shape.index(max(drawn.shape))
    neighbour = place[:longest] + [(place[longest] + 1) % drawn.shape[longest]] + place[longest + 1:]
    return drawn.at[tuple(place)].set(smallest).at[tuple(neighbour)].set(top_value)


def levels(key, shape, cuts, low, top_value):
    level, own = 1.0, jax.random.fold_in(key, 6)
    for dim, blocks in cuts:
        steps = jnp.exp(jax.random.uniform(jax.random.fold_in(own, dim), (blocks,), jnp.float32, low / len(cuts), top_value / len(cuts)))
        level = level * jnp.repeat(steps, shape[dim] // blocks).reshape([-1 if axis == dim else 1 for axis in range(len(shape))])
    return level


def normal_values(own_key, dims, scale, most, pieces=(), held_as=jnp.bfloat16):
    level = levels(own_key, dims, pieces, -0.22, 0.18) if pieces else 1.0
    entries = jax.random.normal(own_key, dims, jnp.float32) * scale * level
    return jnp.minimum(jnp.maximum(entries, -most), most).astype(held_as)


def setup_inputs(seed: int = 0) -> dict:
    splits = jax.random.split(jax.random.key(seed), 10)
    load_source = draw_load_source(jax.random.fold_in(splits[9], 71), 0)
    schur_diag = jnp.clip(jnp.exp(math.log(3.0) - 2.3025851 * jax.random.uniform(splits[1], (GRPS, SUBS, I), jnp.float32) ** levels(splits[1], (GRPS, SUBS, I), ((0, 4), (1, 64)), -0.2, 0.2)), 0.3, 3.0)
    schur_factor = normal_values(splits[2], (GRPS, SUBS, I, I), I ** -0.5, 0.15625, ((0, 4), (1, 64)))
    dir_diag = jnp.clip(jnp.exp(math.log(3.0) - 2.3025851 * jax.random.uniform(splits[3], (GRPS, SUBS, I), jnp.float32) ** levels(splits[3], (GRPS, SUBS, I), ((0, 4), (1, 64)), -0.2, 0.2)), 0.3, 3.0)
    dir_factor = normal_values(splits[4], (GRPS, SUBS, I, I), I ** -0.5, 0.15625, ((0, 4), (1, 64)))
    corner_map = normal_values(splits[5], (GRPS, SUBS, NCR, I), (I // 4) ** -0.5, 0.3125, ((0, 4), (1, 64)))
    corner_row = place_ends(jax.random.randint(splits[6], (GRPS, SUBS, NCR), 0, NC), jax.random.fold_in(splits[6], 1), 0, NC - 1).astype(jnp.int32)
    coarse_factor = normal_values(splits[7], (NC, NC), NC ** -0.5, 0.125, ((0, 256),))
    slot_table = draw_slot_table(jax.random.fold_in(splits[9], 71), 0)
    return dict(load_source=load_source, schur_diag=schur_diag, schur_factor=schur_factor, dir_diag=dir_diag, dir_factor=dir_factor, corner_map=corner_map, corner_row=corner_row, coarse_factor=coarse_factor, slot_table=slot_table)


OFFSETS = (1, 2, 5, -1, -2, -5)
CONTRACT_LAST = (((1,), (1,)), ((), ()))


def take_block(values, indices):
    return jnp.take(values, indices, axis=1, mode="fill", fill_value=0)


def put_block(target, indices, update):
    return target.at[:, indices].set(update, mode="drop")


def jump_all(values, slot_table, live_mask):
    take_many = jax.vmap(jax.vmap(take_block))
    put_many = jax.vmap(jax.vmap(put_block))
    received = jnp.zeros(values.shape, values.dtype)
    for direction in range(6):
        opposite = (direction + 3) % 6
        outgoing = take_many(values, slot_table[:, :, opposite])
        incoming = jnp.roll(outgoing, -OFFSETS[direction], axis=1)
        received = put_many(received, slot_table[:, :, direction], incoming)
    return live_mask[:, :, None, :] * (values.astype(jnp.float32) - received.astype(jnp.float32))


def reference(load_source, schur_diag, schur_factor, dir_diag, dir_factor, corner_map, corner_row, coarse_factor, slot_table):
    groups = load_source.shape[0]
    members = load_source.shape[1]
    cases = load_source.shape[2]
    interface = load_source.shape[3]
    total_subs = groups * members
    coarse_size = coarse_factor.shape[0]

    def flatten_lead(array):
        return array.reshape((total_subs,) + array.shape[2:])

    def restore_lead(array):
        return array.reshape((groups, members) + array.shape[1:])

    def mark_live(indices):
        return jnp.zeros((interface,), jnp.float32).at[indices].set(1.0, mode="drop")

    live_mask = restore_lead(jax.vmap(mark_live)(flatten_lead(slot_table).reshape(total_subs, -1)))

    def precondition(field):
        def single_sub(operands):
            vector, diagonal, factor = operands
            middle = jnp.dot(vector.astype(jnp.bfloat16), factor, preferred_element_type=jnp.float32).astype(jnp.bfloat16)
            back = lax.dot_general(middle, factor, CONTRACT_LAST, preferred_element_type=jnp.float32)
            return (0.5 * (diagonal[None, :] * vector + back)).astype(jnp.bfloat16)
        dir_out = restore_lead(lax.map(single_sub, (flatten_lead(field), flatten_lead(dir_diag), flatten_lead(dir_factor))))
        return 0.5 * jump_all(dir_out, slot_table, live_mask)

    rows_flat = flatten_lead(corner_row)

    def apply_schur(field):
        def first_part(operands):
            vector, diagonal, factor, corner_part = operands
            operand = vector.astype(jnp.bfloat16)
            middle = jnp.dot(operand, factor, preferred_element_type=jnp.float32).astype(jnp.bfloat16)
            local_term = diagonal[None, :] * vector + lax.dot_general(middle, factor, CONTRACT_LAST, preferred_element_type=jnp.float32)
            corner_in = lax.dot_general(operand, corner_part, CONTRACT_LAST, preferred_element_type=jnp.float32)
            return local_term, corner_in
        local_term, corner_in = lax.map(first_part, (flatten_lead(field), flatten_lead(schur_diag), flatten_lead(schur_factor), flatten_lead(corner_map)))
        spread = jnp.transpose(corner_in, (1, 0, 2)).reshape(cases, -1)
        coarse_in = jnp.zeros((cases, coarse_size), jnp.float32).at[:, rows_flat.reshape(-1)].add(spread)
        coarse_middle = jnp.dot(coarse_in.astype(jnp.bfloat16), coarse_factor, preferred_element_type=jnp.float32).astype(jnp.bfloat16)
        coarse_out = lax.dot_general(coarse_middle, coarse_factor, CONTRACT_LAST, preferred_element_type=jnp.float32).astype(jnp.bfloat16)
        picked = jnp.transpose(jnp.take(coarse_out, rows_flat, axis=1), (1, 0, 2))

        def second_part(operands):
            local_one, picked_one, corner_part = operands
            corner_out = jnp.dot(picked_one, corner_part, preferred_element_type=jnp.float32)
            return (local_one + corner_out).astype(jnp.bfloat16)
        schur_out = restore_lead(lax.map(second_part, (local_term, picked, flatten_lead(corner_map))))
        return jump_all(schur_out, slot_table, live_mask)

    def case_sum(field):
        return jnp.sum(field, axis=(0, 1, 3))

    residual = jump_all(load_source, slot_table, live_mask)
    smoothed = precondition(residual)
    product_now = case_sum(residual * smoothed)
    direction = smoothed
    multipliers = jnp.zeros(residual.shape, jnp.float32)
    for step in range(ITERS):
        image = apply_schur(direction)
        step_length = product_now / case_sum(direction * image)
        multipliers = multipliers + step_length[None, None, :, None] * direction
        residual = residual - step_length[None, None, :, None] * image
        if step + 1 < ITERS:
            smoothed = precondition(residual)
            product_next = case_sum(residual * smoothed)
            growth = product_next / product_now
            direction = smoothed + growth[None, None, :, None] * direction
            product_now = product_next
    return multipliers, residual
```

```python
import jax
import jax.numpy as jnp
from jax import lax
from jax.experimental import pallas as pl
from jax.experimental.pallas import tpu as pltpu
from jax.sharding import PartitionSpec as P

OFFSETS = (1, 2, 5, -1, -2, -5)
BLOCKS = len(OFFSETS)
F32 = jnp.float32
BF16 = jnp.bfloat16
LANES = 128


def dot_nn(a, b):
    return jnp.dot(a, b, preferred_element_type=F32)


def dot_nt(a, b):
    return lax.dot_general(a, b, (((1,), (1,)), ((), ())), preferred_element_type=F32)


def dot_tn(a, b):
    return lax.dot_general(a, b, (((0,), (0,)), ((), ())), preferred_element_type=F32)


def column_to_row(column):
    n = column.shape[0]
    same = lax.broadcasted_iota(jnp.int32, (n, n), 0) == lax.broadcasted_iota(jnp.int32, (n, n), 1)
    return jnp.sum(jnp.where(same, column, 0.0), axis=0, keepdims=True)


def row_to_column(row):
    n = row.shape[1]
    same = lax.broadcasted_iota(jnp.int32, (n, n), 0) == lax.broadcasted_iota(jnp.int32, (n, n), 1)
    return jnp.sum(jnp.where(same, row, 0.0), axis=1, keepdims=True)


def three_parts(value):
    first = value.astype(BF16).astype(F32)
    rest = value - first
    second = rest.astype(BF16).astype(F32)
    third = (rest - second).astype(BF16).astype(F32)
    return [first, second, third]


def fold_rows(rows):
    n = rows.shape[0] // 4
    return jnp.concatenate([rows[n * i : n * i + n] for i in range(4)], axis=1)


def unfold_rows(tile):
    n = tile.shape[1] // 4
    return jnp.concatenate([tile[:, n * i : n * i + n] for i in range(4)], axis=0)


def call(body, outs, cost, *args):
    in_vmem = pl.BlockSpec(memory_space=pltpu.VMEM)
    return pl.pallas_call(
        body,
        out_shape=[jax.ShapeDtypeStruct(shape, dtype) for shape, dtype in outs],
        in_specs=[in_vmem] * len(args),
        out_specs=[in_vmem] * len(outs),
        compiler_params=pltpu.CompilerParams(vmem_limit_bytes=40 * 1024 * 1024),
        cost_estimate=pl.CostEstimate(flops=cost, bytes_accessed=cost // 64, transcendentals=0),
    )(*args)


def store_blocks(refs, values, slots_ref):
    cap = refs[0].shape[1]
    for b in range(BLOCKS):
        refs[b][...] = dot_nn(values, slots_ref[:, b * cap : (b + 1) * cap]).astype(BF16)


def first_exchange_body(table_ref, source_ref, slots_ref, *block_refs):
    interface, total = slots_ref.shape
    cap = total // BLOCKS
    rows = lax.broadcasted_iota(jnp.int32, (interface, cap), 0)
    source = source_ref[...]
    for b in range(BLOCKS):
        named = rows == table_ref[0:1, b * cap : (b + 1) * cap]
        block = jnp.where(named, 1.0, 0.0).astype(BF16)
        slots_ref[:, b * cap : (b + 1) * cap] = block
        block_refs[b][...] = dot_nn(source, block).astype(BF16)


def dirichlet_body(*refs):
    incoming = jnp.concatenate([ref[...] for ref in refs[:BLOCKS]], axis=1)
    source_ref, diag_ref, slots_ref, factor_ref = refs[BLOCKS : BLOCKS + 4]
    residual_ref, out_ref, live_ref, rho_ref, *block_refs = refs[BLOCKS + 4 :]
    cases = incoming.shape[0]
    ones = jnp.ones((16, incoming.shape[1]), BF16)
    spread = dot_nt(jnp.concatenate([incoming, ones], axis=0), slots_ref[...])
    live = spread[cases : cases + 8]
    residual = live[0:1] * (source_ref[...].astype(F32) - spread[:cases])
    factor = factor_ref[...]
    middle = dot_nn(residual.astype(BF16), factor).astype(BF16)
    out = (0.5 * (diag_ref[...] * residual + dot_nt(middle, factor))).astype(BF16)
    store_blocks(block_refs, out, slots_ref)
    live_ref[...] = live
    residual_ref[...] = residual
    out_ref[...] = out
    rho = column_to_row(jnp.sum(residual * out.astype(F32), axis=1, keepdims=True))
    rho_ref[...] = jnp.broadcast_to(rho, rho_ref.shape)


def schur_first_body(*refs):
    incoming = jnp.concatenate([ref[...] for ref in refs[:BLOCKS]], axis=1)
    out_ref, live_ref, diag_ref, slots_ref, factor_ref, corner_ref, rho_ref = refs[
        BLOCKS : BLOCKS + 7
    ]
    direction_ref, middle_ref, send_ref = refs[BLOCKS + 7 :]
    received = dot_nt(incoming, slots_ref[...])
    direction = 0.5 * (live_ref[0:1] * (out_ref[...].astype(F32) - received))
    direction_ref[...] = direction
    operand = direction.astype(BF16)
    wide = dot_nn(operand, factor_ref[...])
    middle = wide.astype(BF16)
    middle_ref[...] = middle
    curve = jnp.sum(diag_ref[...] * direction * direction, axis=1, keepdims=True)
    curve = curve + jnp.sum(wide * middle.astype(F32), axis=1, keepdims=True)
    corner_in = dot_nt(corner_ref[...], operand)
    zero = jnp.zeros((2, corner_in.shape[1]), F32)
    scalars = three_parts(rho_ref[0:1]) + three_parts(column_to_row(curve)) + [zero]
    tile = fold_rows(jnp.concatenate([corner_in] + scalars, axis=0)).astype(BF16)
    send_ref[...] = jnp.broadcast_to(tile[None], send_ref.shape)


def schur_second_body(direction_ref, middle_ref, diag_ref, factor_ref, local_ref):
    back = dot_nt(middle_ref[...], factor_ref[...])
    local_ref[...] = diag_ref[...] * direction_ref[...] + back


def deal_columns_body(rows_ref, index_ref, send_ref):
    members, depth, lanes = rows_ref.shape
    group = lax.broadcasted_iota(jnp.int32, (depth, lanes), 1) // 32 % 4
    rows = [rows_ref[a].astype(F32) for a in range(members)]
    index = index_ref[...]
    for t in range(4):
        dealt = jnp.zeros((depth, lanes), F32)
        for a in range(members):
            shift = (32 * (a - t)) % lanes
            moved = pltpu.roll(rows[a], shift, 1) if shift else rows[a]
            dealt = jnp.where(group == a, moved, dealt)
        for quad in range(lanes // LANES):
            send_ref[4 * quad + t, :, :LANES] = dealt[:, quad * LANES : (quad + 1) * LANES].astype(
                BF16
            )
    for other in range(send_ref.shape[0]):
        send_ref[other, :, LANES:] = index


def pick_rows_body(dealt_ref, picked_ref):
    count, depth, _ = dealt_ref.shape
    dealt = dealt_ref[...].astype(F32)
    columns = dealt[:, :, :LANES].reshape(count * depth, LANES).astype(BF16)
    index = dealt[:, :, LANES:].reshape(count * depth, LANES)
    size = count * depth
    place = lax.broadcasted_iota(jnp.int32, (size, size), 1).astype(F32)
    lane_group = (lax.broadcasted_iota(jnp.int32, (size, LANES), 1) // 32).astype(F32)
    near = lax.broadcasted_iota(jnp.int32, (LANES, LANES), 0)
    far = lax.broadcasted_iota(jnp.int32, (LANES, LANES), 1)
    total = jnp.zeros((size, LANES), F32)
    for q in range(3):
        high = index[:, 3 * q : 3 * q + 1] * 8.0 + index[:, 3 * q + 1 : 3 * q + 2]
        onehot = jnp.where(place == high, 1.0, 0.0).astype(BF16)
        rows = dot_nn(onehot, columns)
        rows = jnp.where(lane_group == index[:, 3 * q + 2 : 3 * q + 3], rows, 0.0).astype(BF16)
        fold = jnp.where((near % 32 == far % 32) & (far // 32 == q), 1.0, 0.0).astype(BF16)
        total = total + dot_nn(rows, fold)
    picked_ref[...] = total.astype(BF16)


def coarse_first_body(corner_ref, picked_ref, send_ref):
    count, depth, lanes = corner_ref.shape
    corner = corner_ref[...].astype(F32)
    products = dot_tn(picked_ref[...], corner.reshape(count * depth, lanes).astype(BF16))
    middle = products[:32, :32]
    for q in range(1, 3):
        middle = middle + products[32 * q : 32 * q + 32, 32 * q : 32 * q + 32]
    tile = jnp.concatenate([fold_rows(middle), jnp.sum(corner, axis=0)], axis=0)
    send_ref[...] = jnp.broadcast_to(tile[None], send_ref.shape)


def coarse_second_body(parts_ref, picked_ref, send_ref, totals_ref):
    parts = parts_ref[...]
    total = parts[0]
    for member in range(1, parts.shape[0]):
        total = total + parts[member]
    middle = unfold_rows(total[:8])
    rounded = middle.astype(BF16)
    square = jnp.sum(middle * rounded.astype(F32), axis=0, keepdims=True)
    wide = jnp.concatenate([middle] * 4, axis=1)
    wide = jnp.concatenate([wide] * 4, axis=0)
    near = lax.broadcasted_iota(jnp.int32, wide.shape, 0) // 32
    far = lax.broadcasted_iota(jnp.int32, wide.shape, 1) // 32
    diagonal = jnp.where(near == far, wide, 0.0).astype(BF16)
    out = dot_nn(picked_ref[...], diagonal)
    zero = jnp.zeros((5, 96 // 3), F32)
    scalars = jnp.concatenate(three_parts(square) + [zero], axis=0)
    extra = jnp.concatenate([jnp.zeros((8, 96), F32), scalars], axis=1)
    send_ref[...] = (out.reshape(send_ref.shape) + extra[None]).astype(BF16)
    totals_ref[...] = total[8:16]


def schur_last_body(coarse_ref, totals_ref, local_ref, corner_ref, slots_ref, *out_refs):
    schur_ref, step_ref, *block_refs = out_refs
    summed = jnp.sum(coarse_ref[...].astype(F32), axis=0)
    rows = unfold_rows(summed)
    corners = corner_ref.shape[0]
    picked = rows[:corners].astype(BF16)
    schur = (local_ref[...] + dot_tn(picked, corner_ref[...])).astype(BF16)
    schur_ref[...] = schur
    store_blocks(block_refs, schur, slots_ref)
    square = jnp.sum(rows[corners : corners + 3], axis=0, keepdims=True)
    scalars = totals_ref[:, 96:]
    rho = jnp.sum(scalars[0:3], axis=0, keepdims=True)
    curve = 2.0 * (jnp.sum(scalars[3:6], axis=0, keepdims=True) + square)
    step = row_to_column(rho / curve)
    step_ref[...] = jnp.broadcast_to(step, step_ref.shape)


def update_body(*refs):
    incoming = jnp.concatenate([ref[...] for ref in refs[:BLOCKS]], axis=1)
    schur_ref, step_ref, live_ref, direction_ref, residual_ref, slots_ref = refs[
        BLOCKS : BLOCKS + 6
    ]
    multipliers_ref, new_residual_ref = refs[BLOCKS + 6 :]
    received = dot_nt(incoming, slots_ref[...])
    image = live_ref[0:1] * (schur_ref[...].astype(F32) - received)
    step = step_ref[:, 0:1]
    multipliers_ref[...] = step * direction_ref[...]
    new_residual_ref[...] = residual_ref[...] - step * image


def exchange(blocks):
    count = lax.axis_size("sub")
    received = [None] * BLOCKS
    for b in range(BLOCKS):
        route = [(i, (i + OFFSETS[b]) % count) for i in range(count)]
        received[(b + 3) % BLOCKS] = lax.ppermute(blocks[b], "sub", route)
    return received


def on_device(
    load_source,
    schur_diag,
    schur_factor,
    dir_diag,
    dir_factor,
    corner_map,
    corner_row,
    coarse_factor,
    slot_table,
):
    source = load_source[0, 0]
    schur_factor = schur_factor[0, 0]
    dir_factor = dir_factor[0, 0]
    corner_map = corner_map[0, 0]
    cases, interface = source.shape
    corners = corner_map.shape[0]
    subs, groups = lax.axis_size("sub"), lax.axis_size("grp")
    table = slot_table.reshape(1, -1)
    total = table.shape[1]
    cap = total // BLOCKS
    block_outs = [((cases, cap), BF16)] * BLOCKS
    field = (cases, interface)
    product = 2 * cases * interface * total

    depth, coarse_size = coarse_factor.shape
    rows = lax.all_to_all(
        jnp.broadcast_to(coarse_factor[None], (groups, depth, coarse_size)), "grp", 0, 0, tiled=True
    )
    row = corner_row.reshape(corners // 8, 8)
    index = jnp.stack([row // 32, row % 8, row // 8 % 4], axis=1).reshape(-1, 8).T
    index = jnp.pad(index, ((0, 0), (0, LANES - index.shape[1]))).astype(BF16)

    slots, *blocks = call(
        first_exchange_body, [((interface, total), BF16)] + block_outs, product, table, source
    )
    incoming = exchange(blocks)
    (dealt,) = call(
        deal_columns_body, [((subs, depth, 2 * LANES), BF16)], product // 16, rows, index
    )
    dealt = lax.all_to_all(dealt, "sub", 0, 0, tiled=True)
    residual, dir_out, live, rho, *blocks = call(
        dirichlet_body,
        [(field, F32), (field, BF16), ((8, interface), F32), ((8, cases), F32)] + block_outs,
        4 * product,
        *incoming,
        source,
        dir_diag[0],
        slots,
        dir_factor,
    )
    incoming = exchange(blocks)
    (picked,) = call(pick_rows_body, [((subs * depth, LANES), BF16)], product // 4, dealt)
    direction, schur_middle, corner_in = call(
        schur_first_body,
        [(field, F32), (field, BF16), ((subs, 8, LANES), BF16)],
        2 * product,
        *incoming,
        dir_out,
        live,
        schur_diag[0],
        slots,
        schur_factor,
        corner_map,
        rho,
    )
    corner_in = lax.all_to_all(corner_in, "sub", 0, 0, tiled=True)
    (local,) = call(
        schur_second_body,
        [(field, F32)],
        product,
        direction,
        schur_middle,
        schur_diag[0],
        schur_factor,
    )
    (parts,) = call(
        coarse_first_body, [((groups, 16, LANES), F32)], product // 64, corner_in, picked
    )
    parts = lax.all_to_all(parts, "grp", 0, 0, tiled=True)
    coarse, totals = call(
        coarse_second_body,
        [((subs, 8, LANES), BF16), ((8, LANES), F32)],
        product // 64,
        parts,
        picked,
    )
    coarse = lax.all_to_all(coarse, "sub", 0, 0, tiled=True)
    schur_out, step, *blocks = call(
        schur_last_body,
        [(field, BF16), ((cases, LANES), F32)] + block_outs,
        product,
        coarse,
        totals,
        local,
        corner_map,
        slots,
    )
    incoming = exchange(blocks)
    multipliers, residual = call(
        update_body,
        [(field, F32), (field, F32)],
        product,
        *incoming,
        schur_out,
        step,
        live,
        direction,
        residual,
        slots,
    )
    return (multipliers[None, None], residual[None, None])


def solution(mesh):
    return jax.shard_map(
        on_device,
        mesh=mesh,
        in_specs=(
            P("grp", "sub", None, None),
            P("grp", "sub", None),
            P("grp", "sub", None, None),
            P("grp", "sub", None),
            P("grp", "sub", None, None),
            P("grp", "sub", None, None),
            P("grp", "sub", None),
            P(("sub", "grp"), None),
            P("grp", "sub", None, None),
        ),
        out_specs=(P("grp", "sub", None, None), P("grp", "sub", None, None)),
        check_vma=False,
    )
```

```python
import jax
import jax.numpy as jnp
from jax import lax
from jax.experimental import pallas as pl
from jax.experimental.pallas import tpu as pltpu
from jax.sharding import PartitionSpec as P

OFFSETS = (1, 2, 5, -1, -2, -5)
BLOCKS = len(OFFSETS)
F32 = jnp.float32
BF16 = jnp.bfloat16
LANES = 128
PIECES = 3
TABLE, DIR_DIAG, SCHUR_DIAG, CORNER_ROW = 0, 1, 2, 3


def dot_nn(a, b):
    return jnp.dot(a, b, preferred_element_type=F32)


def dot_nt(a, b):
    return lax.dot_general(a, b, (((1,), (1,)), ((), ())), preferred_element_type=F32)


def dot_tn(a, b):
    return lax.dot_general(a, b, (((0,), (0,)), ((), ())), preferred_element_type=F32)


def column_to_row(column):
    n = column.shape[0]
    same = lax.broadcasted_iota(jnp.int32, (n, n), 0) == lax.broadcasted_iota(jnp.int32, (n, n), 1)
    return jnp.sum(jnp.where(same, column, 0.0), axis=0, keepdims=True)


def row_to_column(row):
    n = row.shape[1]
    same = lax.broadcasted_iota(jnp.int32, (n, n), 0) == lax.broadcasted_iota(jnp.int32, (n, n), 1)
    return jnp.sum(jnp.where(same, row, 0.0), axis=1, keepdims=True)


def three_parts(value):
    first = value.astype(BF16).astype(F32)
    rest = value - first
    second = rest.astype(BF16).astype(F32)
    third = (rest - second).astype(BF16).astype(F32)
    return [first, second, third]


def fold_rows(rows):
    n = rows.shape[0] // 4
    return jnp.concatenate([rows[n * i : n * i + n] for i in range(4)], axis=1)


def unfold_rows(tile):
    n = tile.shape[1] // 4
    return jnp.concatenate([tile[:, n * i : n * i + n] for i in range(4)], axis=0)


def call(body, outs, weight, *args, scratch=(), in_hbm=(), vmem=20):
    in_vmem = pl.BlockSpec(memory_space=pltpu.VMEM)
    left = pl.BlockSpec(memory_space=pltpu.HBM)
    return pl.pallas_call(
        body,
        out_shape=[jax.ShapeDtypeStruct(shape, dtype) for shape, dtype in outs],
        in_specs=[left if i in in_hbm else in_vmem for i in range(len(args))],
        out_specs=[in_vmem] * len(outs),
        scratch_shapes=list(scratch),
        compiler_params=pltpu.CompilerParams(vmem_limit_bytes=vmem * 1024 * 1024),
        cost_estimate=pl.CostEstimate(
            flops=weight << 20, bytes_accessed=weight << 20, transcendentals=0
        ),
    )(*args)


def slot_block(rows_ref, b, interface):
    cap = rows_ref.shape[1] // BLOCKS
    rows = lax.broadcasted_iota(jnp.int32, (interface, cap), 0).astype(F32)
    named = rows == rows_ref[TABLE : TABLE + 1, b * cap : (b + 1) * cap]
    return jnp.where(named, 1.0, 0.0).astype(BF16)


def from_slots(values, rows_ref, b):
    return dot_nn(values, slot_block(rows_ref, b, values.shape[1])).astype(BF16)


def to_slots(blocks, rows_ref, interface):
    total = dot_nt(blocks[0], slot_block(rows_ref, 0, interface))
    for b in range(1, BLOCKS):
        total = total + dot_nt(blocks[b], slot_block(rows_ref, b, interface))
    return total


def share_rows_body(coarse_ref, shared_ref):
    shared_ref[...] = jnp.broadcast_to(coarse_ref[...][None], shared_ref.shape)


def first_exchange_body(rows_ref, fields_ref, *block_refs):
    values = fields_ref[...]
    for b in range(BLOCKS):
        block_refs[b][...] = from_slots(values, rows_ref, b)


def load_factor(factor_ref, held_ref, semaphores):
    size = held_ref.shape[0] // PIECES
    copies = []
    for i in range(PIECES):
        piece = pl.ds(size * i, size)
        copies.append(
            pltpu.make_async_copy(factor_ref.at[piece], held_ref.at[piece], semaphores.at[i])
        )
        copies[i].start()
    return copies


def times_factor(operand, held_ref, copies):
    size = held_ref.shape[0] // PIECES
    total = None
    for i in range(PIECES):
        copies[i].wait()
        part = dot_nn(operand[:, size * i : size * i + size], held_ref[size * i : size * i + size])
        total = part if total is None else total + part
    return total


def dirichlet_body(*refs):
    rows_ref, fields_ref, factor_ref = refs[BLOCKS : BLOCKS + 3]
    residual_ref, out_ref, live_ref, rho_ref, *block_refs = refs[BLOCKS + 3 : -3]
    slots_ref, held_ref, semaphores = refs[-3:]
    copies = load_factor(factor_ref, held_ref, semaphores)
    cases, interface = residual_ref.shape
    cap = block_refs[0].shape[1]
    ones = jnp.ones((16, cap), BF16)
    spread = jnp.zeros((cases + 16, interface), F32)
    for b in range(BLOCKS):
        block = slot_block(rows_ref, b, interface)
        slots_ref[:, b * cap : (b + 1) * cap] = block
        spread = spread + dot_nt(jnp.concatenate([refs[b][:cases], ones], axis=0), block)
    live = spread[cases : cases + 8]
    residual = live[0:1] * (fields_ref[:cases].astype(F32) - spread[:cases])
    middle = times_factor(residual.astype(BF16), held_ref, copies).astype(BF16)
    diag = rows_ref[DIR_DIAG : DIR_DIAG + 1]
    out = (0.5 * (diag * residual + dot_nt(middle, held_ref[...]))).astype(BF16)
    for b in range(BLOCKS):
        block_refs[b][...] = dot_nn(out, slots_ref[:, b * cap : (b + 1) * cap]).astype(BF16)
    live_ref[...] = live
    residual_ref[...] = residual
    out_ref[...] = out
    rho = column_to_row(jnp.sum(residual * out.astype(F32), axis=1, keepdims=True))
    rho_ref[...] = jnp.broadcast_to(rho, rho_ref.shape)


def schur_first_body(*refs):
    out_ref, live_ref, rho_ref, rows_ref, fields_ref, mine_ref, factor_ref = refs[
        BLOCKS : BLOCKS + 7
    ]
    direction_ref, middle_ref, send_ref, held_ref, semaphores = refs[BLOCKS + 7 :]
    copies = load_factor(factor_ref, held_ref, semaphores)
    received = to_slots([ref[...] for ref in refs[:BLOCKS]], rows_ref, out_ref.shape[1])
    direction = 0.5 * (live_ref[0:1] * (out_ref[...].astype(F32) - received))
    direction_ref[...] = direction
    operand = direction.astype(BF16)
    wide = times_factor(operand, held_ref, copies)
    middle = wide.astype(BF16)
    middle_ref[...] = middle
    diag = rows_ref[SCHUR_DIAG : SCHUR_DIAG + 1]
    curve = jnp.sum(diag * direction * direction, axis=1, keepdims=True)
    curve = curve + jnp.sum(wide * middle.astype(F32), axis=1, keepdims=True)
    cases = operand.shape[0]
    corner_in = dot_nt(fields_ref[cases : cases + 24], operand)
    zero = jnp.zeros((2, corner_in.shape[1]), F32)
    scalars = three_parts(rho_ref[0:1]) + three_parts(column_to_row(curve)) + [zero]
    tile = fold_rows(jnp.concatenate([corner_in] + scalars, axis=0)).astype(BF16)
    count, depth, _ = send_ref.shape
    send_ref[:, :, :LANES] = jnp.broadcast_to(tile[None], (count, depth, LANES))
    send_ref[:, :, LANES:] = mine_ref[...]


def flat_tiles(tiles):
    count, depth, lanes = tiles.shape
    return tiles.astype(F32).reshape(count * depth, lanes).astype(BF16)


def schur_second_body(
    direction_ref, middle_ref, rows_ref, factor_ref, local_ref, *rest
):
    block_refs, held_ref, semaphores = rest[:-2], rest[-2], rest[-1]
    for copy in load_factor(factor_ref, held_ref, semaphores):
        copy.wait()
    back = dot_nt(middle_ref[...], held_ref[...])
    diag = rows_ref[SCHUR_DIAG : SCHUR_DIAG + 1]
    local = (diag * direction_ref[...] + back).astype(BF16)
    local_ref[...] = local
    for b in range(BLOCKS):
        block_refs[b][...] = from_slots(local, rows_ref, b)


def index_tile(corner_row, depth):
    corners = corner_row.shape[1]
    row = lax.broadcasted_iota(jnp.int32, (depth, corners), 0)
    lane = lax.broadcasted_iota(jnp.int32, (depth, corners), 1)
    place = lax.broadcasted_iota(jnp.int32, (depth, LANES), 1)
    tile = jnp.zeros((depth, LANES), F32)
    for q in range(3):
        mine = jnp.where(lane == 8 * q + row, corner_row, 0.0)
        value = jnp.sum(mine, axis=1, keepdims=True).astype(jnp.int32)
        parts = (value // 32, value % 8, value // 8 % 4)
        for part in range(3):
            tile = jnp.where(place == 3 * q + part, parts[part].astype(F32), tile)
    return tile.astype(BF16)


def deal(rows, store):
    depth, lanes = rows[0].shape
    group = lax.broadcasted_iota(jnp.int32, (depth, lanes), 1) // 32 % 4
    for t in range(4):
        dealt = jnp.zeros((depth, lanes), F32)
        for a in range(4):
            shift = (32 * (a - t)) % lanes
            moved = pltpu.roll(rows[a], shift, 1) if shift else rows[a]
            dealt = jnp.where(group == a, moved, dealt)
        for quad in range(lanes // LANES):
            store(4 * quad + t, dealt[:, quad * LANES : (quad + 1) * LANES].astype(BF16))


def deal_columns_body(shared_ref, rows_ref, send_ref):
    members, depth, _ = shared_ref.shape
    index = index_tile(rows_ref[CORNER_ROW : CORNER_ROW + 1, :LANES], depth)

    def store(other, tile):
        send_ref[other, :, :LANES] = tile
        send_ref[other, :, LANES:] = index

    deal([shared_ref[a].astype(F32) for a in range(members)], store)


def pick_rows_body(dealt_ref, picked_ref, send_ref):
    count, depth, _ = dealt_ref.shape
    dealt = dealt_ref[...].astype(F32)
    columns = dealt[:, :, :LANES].reshape(count * depth, LANES).astype(BF16)
    index = dealt[:, :, LANES:].reshape(count * depth, LANES)
    size = count * depth
    place = lax.broadcasted_iota(jnp.int32, (size, size), 1).astype(F32)
    lane_group = (lax.broadcasted_iota(jnp.int32, (size, LANES), 1) // 32).astype(F32)
    near = lax.broadcasted_iota(jnp.int32, (LANES, LANES), 0)
    far = lax.broadcasted_iota(jnp.int32, (LANES, LANES), 1)
    total = jnp.zeros((size, LANES), F32)
    for q in range(3):
        high = index[:, 3 * q : 3 * q + 1] * 8.0 + index[:, 3 * q + 1 : 3 * q + 2]
        onehot = jnp.where(place == high, 1.0, 0.0).astype(BF16)
        rows = dot_nn(onehot, columns)
        rows = jnp.where(lane_group == index[:, 3 * q + 2 : 3 * q + 3], rows, 0.0).astype(BF16)
        fold = jnp.where((near % 32 == far % 32) & (far // 32 == q), 1.0, 0.0).astype(BF16)
        total = total + dot_nn(rows, fold)
    picked_ref[...] = total.astype(BF16)

    wide = 32 * count
    source = lax.broadcasted_iota(jnp.int32, (size, wide), 0)
    target = lax.broadcasted_iota(jnp.int32, (size, wide), 1)
    same = (source // 8 == target // 32) & (source % 8 == target % 8)
    turned = dot_tn(index.astype(BF16), jnp.where(same, 1.0, 0.0).astype(BF16))
    slot = lax.broadcasted_iota(jnp.int32, (1, wide), 1) // 8 % 4
    high = jnp.full((1, wide), -1.0, F32)
    part = jnp.full((1, wide), -1.0, F32)
    for q in range(3):
        mine = slot == q
        value = turned[3 * q : 3 * q + 1] * 8.0 + turned[3 * q + 1 : 3 * q + 2]
        high = jnp.where(mine, value, high)
        part = jnp.where(mine, turned[3 * q + 2 : 3 * q + 3], part)
    onehot = jnp.where(source.astype(F32) == high, 1.0, 0.0).astype(BF16)
    spread = dot_tn(columns, onehot)
    chosen = jnp.zeros((32, wide), F32)
    for a in range(4):
        chosen = chosen + jnp.where(part == a, spread[32 * a : 32 * a + 32], 0.0)

    def store(other, tile):
        send_ref[other] = tile

    deal([chosen[8 * a : 8 * a + 8] for a in range(4)], store)


def coarse_first_body(corner_ref, picked_ref, *refs):
    local_refs, send_ref, block_refs = refs[:BLOCKS], refs[BLOCKS], refs[BLOCKS + 1 :]
    count, depth, _ = corner_ref.shape
    corner = corner_ref[:, :, :LANES].astype(F32)
    products = dot_tn(picked_ref[...], corner.reshape(count * depth, LANES).astype(BF16))
    middle = products[:32, :32]
    for q in range(1, 3):
        middle = middle + products[32 * q : 32 * q + 32, 32 * q : 32 * q + 32]
    tile = jnp.concatenate([fold_rows(middle), jnp.sum(corner, axis=0)], axis=0)
    send_ref[...] = jnp.broadcast_to(tile[None], send_ref.shape)
    mine = flat_tiles(corner_ref[:, :, LANES:])
    half = mine.shape[0] // 2
    cases = local_refs[0].shape[0]
    for b in range(BLOCKS):
        block_refs[b][:cases] = local_refs[b][...]
        block_refs[b][cases:, :LANES] = mine[:half]
        block_refs[b][cases:, LANES:] = mine[half:]


def coarse_second_body(parts_ref, send_ref, totals_ref):
    parts = parts_ref[...]
    total = parts[0]
    for member in range(1, parts.shape[0]):
        total = total + parts[member]
    send_ref[...] = jnp.broadcast_to(total[None, :8], send_ref.shape).astype(BF16)
    totals_ref[...] = total[8:16]


def diagonal_sum(products):
    total = products[:32, :32]
    for a in range(1, 4):
        total = total + products[32 * a : 32 * a + 32, 32 * a : 32 * a + 32]
    return total


def update_body(*refs):
    others, firsts = refs[:BLOCKS], refs[BLOCKS : 2 * BLOCKS]
    middle_ref, totals_ref, mine_ref, local_ref = refs[2 * BLOCKS : 2 * BLOCKS + 4]
    rows_ref, fields_ref, live_ref, direction_ref, residual_ref = refs[
        2 * BLOCKS + 4 : 2 * BLOCKS + 9
    ]
    multipliers_ref, new_residual_ref = refs[2 * BLOCKS + 9 :]
    middle = flat_tiles(middle_ref[...])
    half = middle.shape[0] // 2
    cases, interface = local_ref.shape
    corners = 24

    wide = middle.astype(F32)
    square = unfold_rows(jnp.sum(wide * wide, axis=0, keepdims=True))
    square = jnp.sum(square, axis=0, keepdims=True)
    scalars = totals_ref[:, 96:]
    rho = jnp.sum(scalars[0:3], axis=0, keepdims=True)
    curve = 2.0 * (jnp.sum(scalars[3:6], axis=0, keepdims=True) + square)
    step = row_to_column(rho / curve)
    multipliers_ref[...] = step * direction_ref[...]

    picked = diagonal_sum(dot_tn(flat_tiles(mine_ref[:, :, LANES:]), middle))[:corners].astype(BF16)
    schur = (local_ref[...].astype(F32) + dot_tn(picked, fields_ref[cases : cases + corners])).astype(BF16)
    blocks = []
    for b in range(BLOCKS):
        products = dot_tn(others[b][cases:, :LANES], middle[:half])
        products = products + dot_tn(others[b][cases:, LANES:], middle[half:])
        picked = diagonal_sum(products)[:corners].astype(BF16)
        corner_out = dot_tn(picked, firsts[b][cases : cases + corners])
        blocks.append((others[b][:cases].astype(F32) + corner_out).astype(BF16))
    received = to_slots(blocks, rows_ref, interface)
    image = live_ref[0:1] * (schur.astype(F32) - received)
    new_residual_ref[...] = residual_ref[...] - step * image


def exchange(blocks):
    count = lax.axis_size("sub")
    received = [None] * BLOCKS
    for b in range(BLOCKS):
        route = [(i, (i + OFFSETS[b]) % count) for i in range(count)]
        received[(b + 3) % BLOCKS] = lax.ppermute(blocks[b], "sub", route)
    return received


def on_device(
    load_source,
    schur_diag,
    schur_factor,
    dir_diag,
    dir_factor,
    corner_map,
    corner_row,
    coarse_factor,
    slot_table,
):
    source = load_source[0, 0]
    schur_factor = schur_factor[0, 0]
    dir_factor = dir_factor[0, 0]
    cases, interface = source.shape
    subs, groups = lax.axis_size("sub"), lax.axis_size("grp")
    table = slot_table.reshape(1, -1)
    total = table.shape[1]
    cap = total // BLOCKS
    field = (cases, interface)
    depth, coarse_size = coarse_factor.shape
    last_rows = cases + subs * depth // 2

    def blocks_of(rows):
        return [((rows, cap), BF16)] * BLOCKS

    corner_row = corner_row[0].astype(F32)
    corner_row = jnp.pad(corner_row, ((0, 0), (0, interface - corner_row.shape[1])))
    rows = jnp.concatenate([table.astype(F32), dir_diag[0], schur_diag[0], corner_row], axis=0)
    fields = jnp.concatenate([source, corner_map[0, 0]], axis=0)
    fields = jnp.pad(fields, ((0, -fields.shape[0] % 16), (0, 0)))
    first_rows = fields.shape[0]
    factor_scratch = [pltpu.VMEM((interface, interface), BF16), pltpu.SemaphoreType.DMA((PIECES,))]

    (shared,) = call(share_rows_body, [((groups, depth, coarse_size), BF16)], 1, coarse_factor)
    shared = lax.all_to_all(shared, "grp", 0, 0, tiled=True)
    blocks = call(first_exchange_body, blocks_of(first_rows), 4, rows, fields)
    firsts = exchange(blocks)
    (dealt,) = call(
        deal_columns_body, [((subs, depth, 2 * LANES), BF16)], 4, shared, rows
    )
    dealt, *firsts = lax.optimization_barrier((dealt, *firsts))
    dealt = lax.all_to_all(dealt, "sub", 0, 0, tiled=True)
    residual, dir_out, live, rho, *blocks = call(
        dirichlet_body,
        [(field, F32), (field, BF16), ((8, interface), F32), ((8, cases), F32)] + blocks_of(cases),
        16,
        *firsts,
        rows,
        fields,
        dir_factor,
        scratch=[pltpu.VMEM((interface, total), BF16)] + factor_scratch,
        in_hbm=(BLOCKS + 2,),
        vmem=50,
    )
    seconds = exchange(blocks)
    picked, mine = call(
        pick_rows_body,
        [((subs * depth, LANES), BF16), ((subs, depth, LANES), BF16)],
        8,
        dealt,
    )
    direction, schur_middle, corner_in = call(
        schur_first_body,
        [(field, F32), (field, BF16), ((subs, depth, 2 * LANES), BF16)],
        16,
        *seconds,
        dir_out,
        live,
        rho,
        rows,
        fields,
        mine,
        schur_factor,
        scratch=factor_scratch,
        in_hbm=(BLOCKS + 6,),
        vmem=50,
    )
    corner_in = lax.all_to_all(corner_in, "sub", 0, 0, tiled=True)
    local, *blocks = call(
        schur_second_body,
        [(field, BF16)] + blocks_of(cases),
        8,
        direction,
        schur_middle,
        rows,
        schur_factor,
        scratch=factor_scratch,
        in_hbm=(3,),
        vmem=50,
    )
    parts, *blocks = call(
        coarse_first_body,
        [((groups, 16, LANES), F32)] + blocks_of(last_rows),
        4,
        corner_in,
        picked,
        *blocks,
    )
    parts = lax.all_to_all(parts, "grp", 0, 0, tiled=True)
    others = exchange(blocks)
    middle, totals = call(
        coarse_second_body, [((subs, 8, LANES), BF16), ((8, LANES), F32)], 2, parts
    )
    middle = lax.all_to_all(middle, "sub", 0, 0, tiled=True)
    multipliers, residual = call(
        update_body,
        [(field, F32), (field, F32)],
        8,
        *others,
        *firsts,
        middle,
        totals,
        corner_in,
        local,
        rows,
        fields,
        live,
        direction,
        residual,
    )
    return (multipliers[None, None], residual[None, None])


def solution(mesh):
    return jax.shard_map(
        on_device,
        mesh=mesh,
        in_specs=(
            P("grp", "sub", None, None),
            P("grp", "sub", None),
            P("grp", "sub", None, None),
            P("grp", "sub", None),
            P("grp", "sub", None, None),
            P("grp", "sub", None, None),
            P("grp", "sub", None),
            P(("sub", "grp"), None),
            P("grp", "sub", None, None),
        ),
        out_specs=(P("grp", "sub", None, None), P("grp", "sub", None, None)),
        check_vma=False,
    )
```

```python
import jax
import jax.numpy as jnp
from jax import lax
from jax.experimental import pallas as pl
from jax.experimental.pallas import tpu as pltpu
from jax.sharding import PartitionSpec as P

OFFSETS = (1, 2, 5, -1, -2, -5)
BLOCKS = len(OFFSETS)
F32 = jnp.float32
BF16 = jnp.bfloat16
LANES = 128
PIECES = 3
TABLE, DIR_DIAG, SCHUR_DIAG, CORNER_ROW = 0, 1, 2, 3


def dot_nn(a, b):
    return jnp.dot(a, b, preferred_element_type=F32)


def dot_nt(a, b):
    return lax.dot_general(a, b, (((1,), (1,)), ((), ())), preferred_element_type=F32)


def dot_tn(a, b):
    return lax.dot_general(a, b, (((0,), (0,)), ((), ())), preferred_element_type=F32)


def column_to_row(column):
    n = column.shape[0]
    same = lax.broadcasted_iota(jnp.int32, (n, n), 0) == lax.broadcasted_iota(jnp.int32, (n, n), 1)
    return jnp.sum(jnp.where(same, column, 0.0), axis=0, keepdims=True)


def row_to_column(row):
    n = row.shape[1]
    same = lax.broadcasted_iota(jnp.int32, (n, n), 0) == lax.broadcasted_iota(jnp.int32, (n, n), 1)
    return jnp.sum(jnp.where(same, row, 0.0), axis=1, keepdims=True)


def three_parts(value):
    first = value.astype(BF16).astype(F32)
    rest = value - first
    second = rest.astype(BF16).astype(F32)
    third = (rest - second).astype(BF16).astype(F32)
    return [first, second, third]


def fold_rows(rows):
    n = rows.shape[0] // 4
    return jnp.concatenate([rows[n * i : n * i + n] for i in range(4)], axis=1)


def unfold_rows(tile):
    n = tile.shape[1] // 4
    return jnp.concatenate([tile[:, n * i : n * i + n] for i in range(4)], axis=0)


def call(body, outs, weight, *args, scratch=(), in_hbm=(), vmem=20):
    in_vmem = pl.BlockSpec(memory_space=pltpu.VMEM)
    left = pl.BlockSpec(memory_space=pltpu.HBM)
    return pl.pallas_call(
        body,
        out_shape=[jax.ShapeDtypeStruct(shape, dtype) for shape, dtype in outs],
        in_specs=[left if i in in_hbm else in_vmem for i in range(len(args))],
        out_specs=[in_vmem] * len(outs),
        scratch_shapes=list(scratch),
        compiler_params=pltpu.CompilerParams(vmem_limit_bytes=vmem * 1024 * 1024),
        cost_estimate=pl.CostEstimate(
            flops=weight << 20, bytes_accessed=weight << 20, transcendentals=0
        ),
    )(*args)


def slot_block(rows_ref, b, interface):
    cap = rows_ref.shape[1] // BLOCKS
    rows = lax.broadcasted_iota(jnp.int32, (interface, cap), 0).astype(F32)
    named = rows == rows_ref[TABLE : TABLE + 1, b * cap : (b + 1) * cap]
    return jnp.where(named, 1.0, 0.0).astype(BF16)


def from_slots(values, rows_ref, b):
    return dot_nn(values, slot_block(rows_ref, b, values.shape[1])).astype(BF16)


def to_slots(blocks, rows_ref, interface):
    total = dot_nt(blocks[0], slot_block(rows_ref, 0, interface))
    for b in range(1, BLOCKS):
        total = total + dot_nt(blocks[b], slot_block(rows_ref, b, interface))
    return total


def first_exchange_body(rows_ref, fields_ref, *block_refs):
    values = fields_ref[: block_refs[0].shape[0]]
    for b in range(BLOCKS):
        block_refs[b][...] = from_slots(values, rows_ref, b)


def load_factor(factor_ref, held_ref, semaphores):
    size = held_ref.shape[0] // PIECES
    copies = []
    for i in range(PIECES):
        piece = pl.ds(size * i, size)
        copies.append(
            pltpu.make_async_copy(factor_ref.at[piece], held_ref.at[piece], semaphores.at[i])
        )
        copies[i].start()
    return copies


def times_factor(operand, held_ref, copies):
    size = held_ref.shape[0] // PIECES
    total = None
    for i in range(PIECES):
        copies[i].wait()
        part = dot_nn(operand[:, size * i : size * i + size], held_ref[size * i : size * i + size])
        total = part if total is None else total + part
    return total


def dirichlet_body(*refs):
    rows_ref, fields_ref, factor_ref = refs[BLOCKS : BLOCKS + 3]
    residual_ref, out_ref, live_ref, rho_ref, *block_refs = refs[BLOCKS + 3 : -3]
    slots_ref, held_ref, semaphores = refs[-3:]
    copies = load_factor(factor_ref, held_ref, semaphores)
    cases, interface = residual_ref.shape
    cap = block_refs[0].shape[1]
    ones = jnp.ones((16, cap), BF16)
    spread = jnp.zeros((cases + 16, interface), F32)
    for b in range(BLOCKS):
        block = slot_block(rows_ref, b, interface)
        slots_ref[:, b * cap : (b + 1) * cap] = block
        spread = spread + dot_nt(jnp.concatenate([refs[b][:cases], ones], axis=0), block)
    live = spread[cases : cases + 8]
    residual = live[0:1] * (fields_ref[:cases].astype(F32) - spread[:cases])
    middle = times_factor(residual.astype(BF16), held_ref, copies).astype(BF16)
    diag = rows_ref[DIR_DIAG : DIR_DIAG + 1]
    out = (0.5 * (diag * residual + dot_nt(middle, held_ref[...]))).astype(BF16)
    for b in range(BLOCKS):
        block_refs[b][...] = dot_nn(out, slots_ref[:, b * cap : (b + 1) * cap]).astype(BF16)
    live_ref[...] = live
    residual_ref[...] = residual
    out_ref[...] = out
    rho = column_to_row(jnp.sum(residual * out.astype(F32), axis=1, keepdims=True))
    rho_ref[...] = jnp.broadcast_to(rho, rho_ref.shape)


def schur_first_body(*refs):
    out_ref, live_ref, rho_ref, rows_ref, fields_ref, dealt_ref, factor_ref = refs[
        BLOCKS : BLOCKS + 7
    ]
    direction_ref, middle_ref, send_ref, held_ref, semaphores = refs[BLOCKS + 7 :]
    copies = load_factor(factor_ref, held_ref, semaphores)
    received = to_slots([ref[...] for ref in refs[:BLOCKS]], rows_ref, out_ref.shape[1])
    direction = 0.5 * (live_ref[0:1] * (out_ref[...].astype(F32) - received))
    direction_ref[...] = direction
    operand = direction.astype(BF16)
    wide = times_factor(operand, held_ref, copies)
    middle = wide.astype(BF16)
    middle_ref[...] = middle
    diag = rows_ref[SCHUR_DIAG : SCHUR_DIAG + 1]
    curve = jnp.sum(diag * direction * direction, axis=1, keepdims=True)
    curve = curve + jnp.sum(wide * middle.astype(F32), axis=1, keepdims=True)
    cases = operand.shape[0]
    corner_in = dot_nt(fields_ref[cases : cases + 24], operand)
    rho_parts, curve_parts = three_parts(rho_ref[0:1]), three_parts(column_to_row(curve))
    extra = extra_lanes(rho_parts + curve_parts, rows_ref[CORNER_ROW : CORNER_ROW + 1, :LANES])
    groups = [corner_in[0:8], corner_in[8:16], corner_in[16:24], extra]
    tile = jnp.concatenate(groups, axis=1).astype(BF16)
    count, depth, _ = send_ref.shape
    send_ref[:, :, :LANES] = jnp.broadcast_to(tile[None], (count, depth, LANES))
    send_ref[:, :, LANES:] = dealt_ref[...]


def schur_second_body(
    direction_ref, middle_ref, rows_ref, factor_ref, local_ref, held_ref, semaphores
):
    for copy in load_factor(factor_ref, held_ref, semaphores):
        copy.wait()
    back = dot_nt(middle_ref[...], held_ref[...])
    local_ref[...] = rows_ref[SCHUR_DIAG : SCHUR_DIAG + 1] * direction_ref[...] + back


def extra_lanes(parts, corner_row):
    cases, corners = parts[0].shape[1], corner_row.shape[1]
    row = lax.broadcasted_iota(jnp.int32, (8, corners), 0)
    lane = lax.broadcasted_iota(jnp.int32, (8, corners), 1)
    near = lax.broadcasted_iota(jnp.int32, (8, cases), 0)
    far = lax.broadcasted_iota(jnp.int32, (8, cases), 1)
    place = lax.broadcasted_iota(jnp.int32, (8, 32), 1)
    tile = jnp.zeros((8, 32), F32)
    for q in range(3):
        mine = jnp.where(lane == 8 * q + row, corner_row, 0.0)
        value = jnp.sum(mine, axis=1, keepdims=True).astype(jnp.int32)
        tile = jnp.where(place == 2 * q, (value // 8).astype(F32), tile)
        tile = jnp.where(place == 2 * q + 1, (value % 8).astype(F32), tile)
    for p, part in enumerate(parts):
        for j in range(4):
            value = jnp.sum(jnp.where(far == 4 * near + j, part, 0.0), axis=1, keepdims=True)
            tile = jnp.where(place == 8 + 4 * p + j, value, tile)
    return tile


def part_row(tile, p, cases):
    near = lax.broadcasted_iota(jnp.int32, (8, cases), 0)
    far = lax.broadcasted_iota(jnp.int32, (8, cases), 1)
    total = jnp.zeros((8, cases), F32)
    for j in range(4):
        lane = 96 + 8 + 4 * p + j
        total = jnp.where(far == 4 * near + j, tile[:, lane : lane + 1], total)
    return jnp.sum(total, axis=0, keepdims=True)


def deal_columns_body(own_ref, one_ref, two_ref, three_ref, send_ref):
    rows = [ref[...].astype(F32) for ref in (own_ref, one_ref, two_ref, three_ref)]
    depth, lanes = rows[0].shape
    group = lax.broadcasted_iota(jnp.int32, (depth, lanes), 1) // 32 % 4
    for t in range(4):
        dealt = jnp.zeros((depth, lanes), F32)
        for a in range(4):
            shift = (32 * (a - t)) % lanes
            moved = pltpu.roll(rows[a], shift, 1) if shift else rows[a]
            dealt = jnp.where(group == a, moved, dealt)
        for quad in range(lanes // LANES):
            tile = dealt[:, quad * LANES : (quad + 1) * LANES]
            send_ref[4 * quad + t] = tile.astype(BF16)


def coarse_first_body(sent_ref, picked_ref, send_ref):
    count, depth, _ = sent_ref.shape
    size = count * depth
    sent = sent_ref[...].astype(F32)
    tiles = sent[:, :, :LANES]
    corner = tiles.reshape(size, LANES)
    columns = sent[:, :, LANES:].reshape(size, LANES).astype(BF16)
    place = lax.broadcasted_iota(jnp.int32, (size, size), 1).astype(F32)
    lane_group = (lax.broadcasted_iota(jnp.int32, (size, LANES), 1) // 32).astype(F32)
    near = lax.broadcasted_iota(jnp.int32, (LANES, LANES), 0)
    far = lax.broadcasted_iota(jnp.int32, (LANES, LANES), 1)
    total = jnp.zeros((size, LANES), F32)
    for q in range(3):
        upper, lower = corner[:, 96 + 2 * q : 97 + 2 * q], corner[:, 97 + 2 * q : 98 + 2 * q]
        member = jnp.floor(upper * 0.25)
        onehot = jnp.where(place == member * 8.0 + lower, 1.0, 0.0).astype(BF16)
        rows = dot_nn(onehot, columns)
        rows = jnp.where(lane_group == upper - 4.0 * member, rows, 0.0).astype(BF16)
        fold = jnp.where((near % 32 == far % 32) & (far // 32 == q), 1.0, 0.0).astype(BF16)
        total = total + dot_nn(rows, fold)
    picked = total.astype(BF16)
    picked_ref[...] = picked
    products = dot_tn(picked, corner.astype(BF16))
    middle = products[:32, :32]
    for q in range(1, 3):
        middle = middle + products[32 * q : 32 * q + 32, 32 * q : 32 * q + 32]
    send_ref[...] = jnp.concatenate([fold_rows(middle), jnp.sum(tiles, axis=0)], axis=0)


def coarse_second_body(own_ref, one_ref, two_ref, three_ref, picked_ref, send_ref, totals_ref):
    total = (own_ref[...] + two_ref[...]) + (one_ref[...] + three_ref[...])
    middle = unfold_rows(total[:8])
    rounded = middle.astype(BF16)
    square = jnp.sum(middle * rounded.astype(F32), axis=0, keepdims=True)
    wide = jnp.concatenate([middle] * 4, axis=1)
    wide = jnp.concatenate([wide] * 4, axis=0)
    near = lax.broadcasted_iota(jnp.int32, wide.shape, 0) // 32
    far = lax.broadcasted_iota(jnp.int32, wide.shape, 1) // 32
    diagonal = jnp.where(near == far, wide, 0.0).astype(BF16)
    out = dot_nn(picked_ref[...], diagonal)
    zero = jnp.zeros((5, 96 // 3), F32)
    scalars = jnp.concatenate(three_parts(square) + [zero], axis=0)
    extra = jnp.concatenate([jnp.zeros((8, 96), F32), scalars], axis=1)
    send_ref[...] = (out.reshape(send_ref.shape) + extra[None]).astype(BF16)
    totals_ref[...] = total[8:16]


def schur_last_body(coarse_ref, totals_ref, local_ref, fields_ref, rows_ref, *out_refs):
    schur_ref, step_ref, *block_refs = out_refs
    cases = local_ref.shape[0]
    rows = unfold_rows(jnp.sum(coarse_ref[...].astype(F32), axis=0))
    picked = rows[:24].astype(BF16)
    schur = local_ref[...] + dot_tn(picked, fields_ref[cases : cases + 24])
    schur = schur.astype(BF16)
    schur_ref[...] = schur
    for b in range(BLOCKS):
        block_refs[b][...] = from_slots(schur, rows_ref, b)
    square = jnp.sum(rows[24:27], axis=0, keepdims=True)
    parts = [part_row(totals_ref[...], p, cases) for p in range(6)]
    rho = parts[0] + parts[1] + parts[2]
    curve = 2.0 * (parts[3] + parts[4] + parts[5] + square)
    step_ref[...] = jnp.broadcast_to(row_to_column(rho / curve), step_ref.shape)


def update_body(*refs):
    schur_ref, step_ref, live_ref, direction_ref, residual_ref, rows_ref = refs[
        BLOCKS : BLOCKS + 6
    ]
    multipliers_ref, new_residual_ref = refs[BLOCKS + 6 :]
    received = to_slots([ref[...] for ref in refs[:BLOCKS]], rows_ref, schur_ref.shape[1])
    image = live_ref[0:1] * (schur_ref[...].astype(F32) - received)
    step = step_ref[:, 0:1]
    multipliers_ref[...] = step * direction_ref[...]
    new_residual_ref[...] = residual_ref[...] - step * image


def exchange(blocks):
    count = lax.axis_size("sub")
    received = [None] * BLOCKS
    for b in (2, 5, 1, 4, 0, 3):
        route = [(i, (i + OFFSETS[b]) % count) for i in range(count)]
        received[(b + 3) % BLOCKS] = lax.ppermute(blocks[b], "sub", route)
    return received


def to_groups(block):
    count = lax.axis_size("grp")
    return [
        lax.ppermute(block, "grp", [(i, (i + k) % count) for i in range(count)])
        for k in range(1, count)
    ]


def on_device(
    load_source,
    schur_diag,
    schur_factor,
    dir_diag,
    dir_factor,
    corner_map,
    corner_row,
    coarse_factor,
    slot_table,
):
    source = load_source[0, 0]
    schur_factor = schur_factor[0, 0]
    dir_factor = dir_factor[0, 0]
    cases, interface = source.shape
    subs, groups = lax.axis_size("sub"), lax.axis_size("grp")
    table = slot_table.reshape(1, -1)
    total = table.shape[1]
    cap = total // BLOCKS
    field = (cases, interface)
    depth, coarse_size = coarse_factor.shape

    def blocks_of(rows):
        return [((rows, cap), BF16)] * BLOCKS

    corner = corner_row[0]
    away = (lax.axis_index("grp") - corner // 8 % 4) % groups
    corner = ((corner // 32 * 4 + away) * 8 + corner % 8).astype(F32)
    corner_row = jnp.pad(corner, ((0, 0), (0, interface - corner.shape[1])))
    rows = jnp.concatenate([table.astype(F32), dir_diag[0], schur_diag[0], corner_row], axis=0)
    fields = jnp.concatenate([source, corner_map[0, 0]], axis=0)
    fields = jnp.pad(fields, ((0, -fields.shape[0] % 16), (0, 0)))
    factor_scratch = [pltpu.VMEM((interface, interface), BF16), pltpu.SemaphoreType.DMA((PIECES,))]

    coarse_rows = [coarse_factor] + to_groups(coarse_factor)
    blocks = call(first_exchange_body, blocks_of(cases), 4, rows, fields)
    firsts = exchange(blocks)
    residual, dir_out, live, rho, *blocks = call(
        dirichlet_body,
        [(field, F32), (field, BF16), ((8, interface), F32), ((8, cases), F32)] + blocks_of(cases),
        16,
        *firsts,
        rows,
        fields,
        dir_factor,
        scratch=[pltpu.VMEM((interface, total), BF16)] + factor_scratch,
        in_hbm=(BLOCKS + 2,),
        vmem=50,
    )
    seconds = exchange(blocks)
    *coarse_rows, rho = lax.optimization_barrier((*coarse_rows, rho))
    (dealt,) = call(deal_columns_body, [((subs, depth, LANES), BF16)], 2, *coarse_rows)
    direction, schur_middle, corner_in = call(
        schur_first_body,
        [(field, F32), (field, BF16), ((subs, depth, 2 * LANES), BF16)],
        16,
        *seconds,
        dir_out,
        live,
        rho,
        rows,
        fields,
        dealt,
        schur_factor,
        scratch=factor_scratch,
        in_hbm=(BLOCKS + 6,),
        vmem=50,
    )
    corner_in = lax.all_to_all(corner_in, "sub", 0, 0, tiled=True)
    (local,) = call(
        schur_second_body,
        [(field, F32)],
        8,
        direction,
        schur_middle,
        rows,
        schur_factor,
        scratch=factor_scratch,
        in_hbm=(3,),
        vmem=50,
    )
    picked, parts = call(
        coarse_first_body,
        [((subs * depth, LANES), BF16), ((16, LANES), F32)],
        4,
        corner_in,
    )
    local, parts = lax.optimization_barrier((local, parts))
    coarse, totals = call(
        coarse_second_body,
        [((subs, 8, LANES), BF16), ((8, LANES), F32)],
        2,
        parts,
        *to_groups(parts),
        picked,
    )
    coarse = lax.all_to_all(coarse, "sub", 0, 0, tiled=True)
    schur_out, step, *blocks = call(
        schur_last_body,
        [(field, BF16), ((cases, LANES), F32)] + blocks_of(cases),
        8,
        coarse,
        totals,
        local,
        fields,
        rows,
    )
    multipliers, residual = call(
        update_body,
        [(field, F32), (field, F32)],
        8,
        *exchange(blocks),
        schur_out,
        step,
        live,
        direction,
        residual,
        rows,
    )
    return (multipliers[None, None], residual[None, None])


def solution(mesh):
    return jax.shard_map(
        on_device,
        mesh=mesh,
        in_specs=(
            P("grp", "sub", None, None),
            P("grp", "sub", None),
            P("grp", "sub", None, None),
            P("grp", "sub", None),
            P("grp", "sub", None, None),
            P("grp", "sub", None, None),
            P("grp", "sub", None),
            P(("sub", "grp"), None),
            P("grp", "sub", None, None),
        ),
        out_specs=(P("grp", "sub", None, None), P("grp", "sub", None, None)),
        check_vma=False,
    )
```

```python
import jax
import jax.numpy as jnp
from jax import lax
from jax.experimental import pallas as pl
from jax.experimental.pallas import tpu as pltpu
from jax.sharding import PartitionSpec as P

OFFSETS = (1, 2, 5, -1, -2, -5)
BLOCKS = len(OFFSETS)
F32 = jnp.float32
BF16 = jnp.bfloat16
LANES = 128
PIECES = 3
RECEIVE_ORDER = (2, 1, 0, 5, 4, 3)
TABLE, DIR_DIAG, SCHUR_DIAG = 0, 1, 2


def dot_nn(a, b):
    return jnp.dot(a, b, preferred_element_type=F32)


def dot_nt(a, b):
    return lax.dot_general(a, b, (((1,), (1,)), ((), ())), preferred_element_type=F32)


def dot_tn(a, b):
    return lax.dot_general(a, b, (((0,), (0,)), ((), ())), preferred_element_type=F32)


def column_to_row(column):
    n = column.shape[0]
    same = lax.broadcasted_iota(jnp.int32, (n, n), 0) == lax.broadcasted_iota(jnp.int32, (n, n), 1)
    return jnp.sum(jnp.where(same, column, 0.0), axis=0, keepdims=True)


def row_to_column(row):
    n = row.shape[1]
    same = lax.broadcasted_iota(jnp.int32, (n, n), 0) == lax.broadcasted_iota(jnp.int32, (n, n), 1)
    return jnp.sum(jnp.where(same, row, 0.0), axis=1, keepdims=True)


def three_parts(value):
    first = value.astype(BF16).astype(F32)
    rest = value - first
    second = rest.astype(BF16).astype(F32)
    third = (rest - second).astype(BF16).astype(F32)
    return [first, second, third]


def fold_rows(rows):
    n = rows.shape[0] // 4
    return jnp.concatenate([rows[n * i : n * i + n] for i in range(4)], axis=1)


def unfold_rows(tile):
    n = tile.shape[1] // 4
    return jnp.concatenate([tile[:, n * i : n * i + n] for i in range(4)], axis=0)


def call(body, outs, weight, *args, scratch=(), in_hbm=(), vmem=20):
    in_vmem = pl.BlockSpec(memory_space=pltpu.VMEM)
    left = pl.BlockSpec(memory_space=pltpu.HBM)
    return pl.pallas_call(
        body,
        out_shape=[jax.ShapeDtypeStruct(shape, dtype) for shape, dtype in outs],
        in_specs=[left if i in in_hbm else in_vmem for i in range(len(args))],
        out_specs=[in_vmem] * len(outs),
        scratch_shapes=list(scratch),
        compiler_params=pltpu.CompilerParams(vmem_limit_bytes=vmem * 1024 * 1024),
        cost_estimate=pl.CostEstimate(
            flops=weight << 20, bytes_accessed=weight << 20, transcendentals=0
        ),
    )(*args)


def at_slots(values, table, b):
    cap, interface = table.shape[1] // BLOCKS, values.shape[1]
    slot = lax.broadcasted_iota(jnp.int32, (interface, cap), 0).astype(F32)
    named = slot == table[:, b * cap : (b + 1) * cap]
    return dot_nn(values, jnp.where(named, 1.0, 0.0).astype(BF16))


def from_slots(values, table, b):
    return at_slots(values, table, b).astype(BF16)


def to_slots(blocks, columns_ref, interface):
    slot = lax.broadcasted_iota(jnp.int32, (columns_ref.shape[0], interface), 1).astype(F32)
    total = None
    for block, b in zip(blocks, RECEIVE_ORDER):
        named = slot == columns_ref[:, b : b + 1]
        part = dot_nn(block, jnp.where(named, 1.0, 0.0).astype(BF16))
        total = part if total is None else total + part
    return total


def first_exchange_body(rows_ref, fields_ref, columns_ref, *block_refs):
    cases, cap = block_refs[0].shape
    table = rows_ref[TABLE : TABLE + 1]
    for b in range(BLOCKS):
        block_refs[b][...] = from_slots(fields_ref[:cases], table, b)
    lane = lax.broadcasted_iota(jnp.int32, columns_ref.shape, 1)
    columns = jnp.zeros(columns_ref.shape, F32)
    for b in range(BLOCKS):
        column = row_to_column(table[:, b * cap : (b + 1) * cap])
        columns = jnp.where(lane == b, column, columns)
    columns_ref[...] = columns


def load_factor(factor_ref, held_ref, semaphores):
    size = held_ref.shape[0] // PIECES
    copies = []
    for i in range(PIECES):
        piece = pl.ds(size * i, size)
        copies.append(
            pltpu.make_async_copy(factor_ref.at[piece], held_ref.at[piece], semaphores.at[i])
        )
        copies[i].start()
    return copies


def times_factor(operand, held_ref, copies):
    size = held_ref.shape[0] // PIECES
    total = None
    for i in range(PIECES):
        copies[i].wait()
        part = dot_nn(operand[:, size * i : size * i + size], held_ref[size * i : size * i + size])
        total = part if total is None else total + part
    return total


def dirichlet_body(*refs):
    columns_ref, rows_ref, fields_ref, factor_ref = refs[BLOCKS : BLOCKS + 4]
    residual_ref, out_ref, live_ref, rho_ref, *block_refs = refs[BLOCKS + 4 : -2]
    held_ref, semaphores = refs[-2:]
    copies = load_factor(factor_ref, held_ref, semaphores)
    cases, interface = residual_ref.shape
    ones = jnp.ones((16, block_refs[0].shape[1]), BF16)
    blocks = [jnp.concatenate([ref[...], ones], axis=0) for ref in refs[:BLOCKS]]
    spread = to_slots(blocks, columns_ref, interface)
    live = spread[cases : cases + 8]
    residual = live[0:1] * (fields_ref[:cases].astype(F32) - spread[:cases])
    middle = times_factor(residual.astype(BF16), held_ref, copies).astype(BF16)
    diag = rows_ref[DIR_DIAG : DIR_DIAG + 1]
    out = (0.5 * (diag * residual + dot_nt(middle, held_ref[...]))).astype(BF16)
    table = rows_ref[TABLE : TABLE + 1]
    for b in range(BLOCKS):
        block_refs[b][...] = from_slots(out, table, b)
    live_ref[...] = live
    residual_ref[...] = residual
    out_ref[...] = out
    rho = column_to_row(jnp.sum(residual * out.astype(F32), axis=1, keepdims=True))
    rho_ref[...] = jnp.broadcast_to(rho, rho_ref.shape)


def schur_first_body(*refs):
    out_ref, live_ref, columns_ref, fields_ref, index_ref, dealt_ref = refs[BLOCKS : BLOCKS + 6]
    direction_ref, send_ref = refs[BLOCKS + 6 :]
    cases, interface = out_ref.shape
    received = to_slots([ref[...] for ref in refs[:BLOCKS]], columns_ref, interface)
    direction = 0.5 * (live_ref[0:1] * (out_ref[...].astype(F32) - received))
    direction_ref[...] = direction
    corner_in = dot_nt(fields_ref[cases : cases + 24], direction.astype(BF16))
    groups = [corner_in[0:8], corner_in[8:16], corner_in[16:24], index_lanes(index_ref[...])]
    tile = jnp.concatenate(groups, axis=1).astype(BF16)
    count, depth, _ = send_ref.shape
    send_ref[:, :, :LANES] = jnp.broadcast_to(tile[None], (count, depth, LANES))
    send_ref[:, :, LANES:] = dealt_ref[...]


def schur_second_body(
    direction_ref,
    rho_ref,
    rows_ref,
    fields_ref,
    factor_ref,
    local_ref,
    sent_ref,
    maps_ref,
    scalars_ref,
    held_ref,
    semaphores,
):
    copies = load_factor(factor_ref, held_ref, semaphores)
    direction = direction_ref[...]
    wide = times_factor(direction.astype(BF16), held_ref, copies)
    middle = wide.astype(BF16)
    scaled = rows_ref[SCHUR_DIAG : SCHUR_DIAG + 1] * direction
    local = scaled + dot_nt(middle, held_ref[...])
    local_ref[...] = local
    cases, interface = local.shape
    values = [part.astype(BF16) for part in three_parts(local)] + [fields_ref[cases:]]
    values = jnp.concatenate(values, axis=0)
    cap = interface // BLOCKS
    for b in range(BLOCKS):
        picked = at_slots(values, rows_ref[TABLE : TABLE + 1], b)
        exact = (picked[:cases] + picked[cases : 2 * cases]) + picked[2 * cases : 3 * cases]
        sent_ref[:, b * cap : (b + 1) * cap] = exact
        maps_ref[:, b * cap : (b + 1) * cap] = picked[3 * cases :].astype(BF16)
    curve = jnp.sum(scaled * direction, axis=1, keepdims=True)
    curve = curve + jnp.sum(wide * middle.astype(F32), axis=1, keepdims=True)
    scalars = [rho_ref[0:1], column_to_row(curve), jnp.zeros((6, curve.shape[0]), F32)]
    scalars = jnp.concatenate(scalars, axis=0)
    scalars_ref[...] = jnp.concatenate([scalars, jnp.zeros((8, 96), F32)], axis=1)


def index_lanes(corner_row):
    corners = corner_row.shape[1]
    row = lax.broadcasted_iota(jnp.int32, (8, corners), 0)
    lane = lax.broadcasted_iota(jnp.int32, (8, corners), 1)
    place = lax.broadcasted_iota(jnp.int32, (8, 32), 1)
    tile = jnp.zeros((8, 32), F32)
    for q in range(3):
        mine = jnp.where(lane == 8 * q + row, corner_row, 0.0)
        value = jnp.sum(mine, axis=1, keepdims=True).astype(jnp.int32)
        tile = jnp.where(place == 2 * q, (value // 8).astype(F32), tile)
        tile = jnp.where(place == 2 * q + 1, (value % 8).astype(F32), tile)
    return tile


def deal_columns_body(own_ref, one_ref, two_ref, three_ref, send_ref):
    rows = [ref[...].astype(F32) for ref in (own_ref, one_ref, two_ref, three_ref)]
    depth, lanes = rows[0].shape
    group = lax.broadcasted_iota(jnp.int32, (depth, lanes), 1) // 32 % 4
    for t in range(4):
        dealt = jnp.zeros((depth, lanes), F32)
        for a in range(4):
            shift = (32 * (a - t)) % lanes
            moved = pltpu.roll(rows[a], shift, 1) if shift else rows[a]
            dealt = jnp.where(group == a, moved, dealt)
        for quad in range(lanes // LANES):
            tile = dealt[:, quad * LANES : (quad + 1) * LANES]
            send_ref[4 * quad + t] = tile.astype(BF16)


def coarse_first_body(sent_ref, scalars_ref, picked_ref, send_ref):
    count, depth, _ = sent_ref.shape
    size = count * depth
    sent = sent_ref[...].astype(F32)
    corner = sent[:, :, :LANES].reshape(size, LANES)
    columns = sent[:, :, LANES:].reshape(size, LANES).astype(BF16)
    place = lax.broadcasted_iota(jnp.int32, (size, size), 1).astype(F32)
    lane_group = (lax.broadcasted_iota(jnp.int32, (size, LANES), 1) // 32).astype(F32)
    near = lax.broadcasted_iota(jnp.int32, (LANES, LANES), 0)
    far = lax.broadcasted_iota(jnp.int32, (LANES, LANES), 1)
    total = jnp.zeros((size, LANES), F32)
    for q in range(3):
        upper, lower = corner[:, 96 + 2 * q : 97 + 2 * q], corner[:, 97 + 2 * q : 98 + 2 * q]
        member = jnp.floor(upper * 0.25)
        onehot = jnp.where(place == member * 8.0 + lower, 1.0, 0.0).astype(BF16)
        rows = dot_nn(onehot, columns)
        rows = jnp.where(lane_group == upper - 4.0 * member, rows, 0.0).astype(BF16)
        fold = jnp.where((near % 32 == far % 32) & (far // 32 == q), 1.0, 0.0).astype(BF16)
        total = total + dot_nn(rows, fold)
    picked = total.astype(BF16)
    picked_ref[...] = picked
    products = dot_tn(picked, corner.astype(BF16))
    middle = products[:32, :32]
    for q in range(1, 3):
        middle = middle + products[32 * q : 32 * q + 32, 32 * q : 32 * q + 32]
    send_ref[...] = jnp.concatenate([fold_rows(middle), scalars_ref[...]], axis=0)


def coarse_second_body(own_ref, one_ref, two_ref, three_ref, picked_ref, send_ref):
    total = (own_ref[...] + two_ref[...]) + (one_ref[...] + three_ref[...])
    middle = unfold_rows(total[:8])
    rounded = middle.astype(BF16)
    square = jnp.sum(middle * rounded.astype(F32), axis=0, keepdims=True)
    wide = jnp.concatenate([middle] * 4, axis=1)
    wide = jnp.concatenate([wide] * 4, axis=0)
    near = lax.broadcasted_iota(jnp.int32, wide.shape, 0) // 32
    far = lax.broadcasted_iota(jnp.int32, wide.shape, 1) // 32
    diagonal = jnp.where(near == far, wide, 0.0).astype(BF16)
    out = dot_nn(picked_ref[...], diagonal)
    rho, curve = total[8:9, :32], total[9:10, :32] + square
    zero = jnp.zeros((2, 32), F32)
    scalars = jnp.concatenate(three_parts(rho) + three_parts(curve) + [zero], axis=0)
    extra = jnp.concatenate([jnp.zeros((8, 96), F32), scalars], axis=1)
    send_ref[...] = (out.reshape(send_ref.shape) + extra[None]).astype(BF16)


def schur_last_body(coarse_ref, local_ref, fields_ref, sent_ref, maps_ref, *out_refs):
    schur_ref, step_ref, *block_refs = out_refs
    cases = local_ref.shape[0]
    rows = unfold_rows(jnp.sum(coarse_ref[...].astype(F32), axis=0))
    picked = rows[:24].astype(BF16)
    cap = block_refs[0].shape[1]
    blocks = (sent_ref[...] + dot_tn(picked, maps_ref[:24])).astype(BF16)
    for b in range(BLOCKS):
        block_refs[b][...] = blocks[:, b * cap : (b + 1) * cap]
    schur = local_ref[...] + dot_tn(picked, fields_ref[cases : cases + 24])
    schur_ref[...] = schur.astype(BF16)
    rho = jnp.sum(rows[24:27], axis=0, keepdims=True)
    curve = 2.0 * jnp.sum(rows[27:30], axis=0, keepdims=True)
    step_ref[...] = jnp.broadcast_to(row_to_column(rho / curve), step_ref.shape)


def update_body(*refs):
    schur_ref, step_ref, live_ref, direction_ref, residual_ref, columns_ref = refs[
        BLOCKS : BLOCKS + 6
    ]
    multipliers_ref, new_residual_ref = refs[BLOCKS + 6 :]
    multipliers_ref[...] = step_ref[:, 0:1] * direction_ref[...]
    received = to_slots([ref[...] for ref in refs[:BLOCKS]], columns_ref, schur_ref.shape[1])
    image = live_ref[0:1] * (schur_ref[...].astype(F32) - received)
    new_residual_ref[...] = residual_ref[...] - step_ref[:, 0:1] * image


def exchange(blocks):
    count = lax.axis_size("sub")
    received = [None] * BLOCKS
    for b in range(BLOCKS):
        route = [(i, (i + OFFSETS[b]) % count) for i in range(count)]
        received[(b + 3) % BLOCKS] = lax.ppermute(blocks[b], "sub", route)
    return [received[b] for b in RECEIVE_ORDER]


def to_groups(block):
    count = lax.axis_size("grp")
    return [
        lax.ppermute(block, "grp", [(i, (i + k) % count) for i in range(count)])
        for k in range(1, count)
    ]


def on_device(
    load_source,
    schur_diag,
    schur_factor,
    dir_diag,
    dir_factor,
    corner_map,
    corner_row,
    coarse_factor,
    slot_table,
):
    source = load_source[0, 0]
    schur_factor = schur_factor[0, 0]
    dir_factor = dir_factor[0, 0]
    cases, interface = source.shape
    subs, groups = lax.axis_size("sub"), lax.axis_size("grp")
    table = slot_table.reshape(1, -1)
    total = table.shape[1]
    cap = total // BLOCKS
    field = (cases, interface)
    depth, coarse_size = coarse_factor.shape

    def blocks_of(rows):
        return [((rows, cap), BF16)] * BLOCKS

    coarse_rows = [coarse_factor] + to_groups(coarse_factor)
    rows = jnp.concatenate([table.astype(F32), dir_diag[0], schur_diag[0]], axis=0)
    fields = jnp.concatenate([source, corner_map[0, 0]], axis=0)
    fields = jnp.pad(fields, ((0, -fields.shape[0] % 16), (0, 0)))
    columns, *blocks = call(
        first_exchange_body, [((cap, LANES), F32)] + blocks_of(cases), 4, rows, fields
    )
    factor_scratch = [pltpu.VMEM((interface, interface), BF16), pltpu.SemaphoreType.DMA((PIECES,))]
    firsts = exchange(blocks)
    residual, dir_out, live, rho, *blocks = call(
        dirichlet_body,
        [(field, F32), (field, BF16), ((8, interface), F32), ((8, cases), F32)] + blocks_of(cases),
        16,
        *firsts,
        columns,
        rows,
        fields,
        dir_factor,
        scratch=factor_scratch,
        in_hbm=(BLOCKS + 3,),
        vmem=50,
    )
    seconds = exchange(blocks)
    *coarse_rows, corner, rho = lax.optimization_barrier((*coarse_rows, corner_row[0], rho))
    away = (lax.axis_index("grp") - corner // 8 % 4) % groups
    corner = ((corner // 32 * 4 + away) * 8 + corner % 8).astype(F32)
    corner = jnp.pad(corner, ((0, 0), (0, LANES - corner.shape[1])))
    (dealt,) = call(deal_columns_body, [((subs, depth, LANES), BF16)], 2, *coarse_rows)
    direction, corner_in = call(
        schur_first_body,
        [(field, F32), ((subs, depth, 2 * LANES), BF16)],
        16,
        *seconds,
        dir_out,
        live,
        columns,
        fields,
        corner,
        dealt,
    )
    corner_in = lax.all_to_all(corner_in, "sub", 0, 0, tiled=True)
    spare = fields.shape[0] - cases
    local, sent, maps, scalars = call(
        schur_second_body,
        [(field, F32), (field, F32), ((spare, total), BF16), ((8, LANES), F32)],
        8,
        direction,
        rho,
        rows,
        fields,
        schur_factor,
        scratch=factor_scratch,
        in_hbm=(4,),
        vmem=50,
    )
    picked, parts = call(
        coarse_first_body,
        [((subs * depth, LANES), BF16), ((16, LANES), F32)],
        4,
        corner_in,
        scalars,
    )
    local, parts = lax.optimization_barrier((local, parts))
    (coarse,) = call(
        coarse_second_body,
        [((subs, 8, LANES), BF16)],
        2,
        parts,
        *to_groups(parts),
        picked,
    )
    coarse = lax.all_to_all(coarse, "sub", 0, 0, tiled=True)
    schur_out, step, *blocks = call(
        schur_last_body,
        [(field, BF16), ((cases, LANES), F32)] + blocks_of(cases),
        8,
        coarse,
        local,
        fields,
        sent,
        maps,
    )
    multipliers, residual = call(
        update_body,
        [(field, F32), (field, F32)],
        8,
        *exchange(blocks),
        schur_out,
        step,
        live,
        direction,
        residual,
        columns,
    )
    return (multipliers[None, None], residual[None, None])


def solution(mesh):
    return jax.shard_map(
        on_device,
        mesh=mesh,
        in_specs=(
            P("grp", "sub", None, None),
            P("grp", "sub", None),
            P("grp", "sub", None, None),
            P("grp", "sub", None),
            P("grp", "sub", None, None),
            P("grp", "sub", None, None),
            P("grp", "sub", None),
            P(("sub", "grp"), None),
            P("grp", "sub", None, None),
        ),
        out_specs=(P("grp", "sub", None, None), P("grp", "sub", None, None)),
        check_vma=False,
    )
```

```python
import jax
import jax.numpy as jnp
from jax import lax
from jax.experimental import pallas as pl
from jax.experimental.pallas import tpu as pltpu
from jax.sharding import PartitionSpec as P

OFFSETS = (1, 2, 5, -1, -2, -5)
BLOCKS = len(OFFSETS)
F32 = jnp.float32
BF16 = jnp.bfloat16
LANES = 128
PIECES = 6
RECEIVE_ORDER = (2, 1, 0, 5, 4, 3)
TABLE, DIR_DIAG, SCHUR_DIAG = 0, 1, 2


def dot_nn(a, b):
    return jnp.dot(a, b, preferred_element_type=F32)


def dot_nt(a, b):
    return lax.dot_general(a, b, (((1,), (1,)), ((), ())), preferred_element_type=F32)


def dot_tn(a, b):
    return lax.dot_general(a, b, (((0,), (0,)), ((), ())), preferred_element_type=F32)


def column_to_row(column):
    n = column.shape[0]
    same = lax.broadcasted_iota(jnp.int32, (n, n), 0) == lax.broadcasted_iota(jnp.int32, (n, n), 1)
    return jnp.sum(jnp.where(same, column, 0.0), axis=0, keepdims=True)


def row_to_column(row):
    n = row.shape[1]
    same = lax.broadcasted_iota(jnp.int32, (n, n), 0) == lax.broadcasted_iota(jnp.int32, (n, n), 1)
    return jnp.sum(jnp.where(same, row, 0.0), axis=1, keepdims=True)


def three_parts(value):
    first = value.astype(BF16).astype(F32)
    rest = value - first
    second = rest.astype(BF16).astype(F32)
    third = (rest - second).astype(BF16).astype(F32)
    return [first, second, third]


def fold_rows(rows):
    n = rows.shape[0] // 4
    return jnp.concatenate([rows[n * i : n * i + n] for i in range(4)], axis=1)


def unfold_rows(tile):
    n = tile.shape[1] // 4
    return jnp.concatenate([tile[:, n * i : n * i + n] for i in range(4)], axis=0)


def call(body, outs, weight, *args, scratch=(), in_hbm=(), vmem=20):
    in_vmem = pl.BlockSpec(memory_space=pltpu.VMEM)
    left = pl.BlockSpec(memory_space=pltpu.HBM)
    return pl.pallas_call(
        body,
        out_shape=[jax.ShapeDtypeStruct(shape, dtype) for shape, dtype in outs],
        in_specs=[left if i in in_hbm else in_vmem for i in range(len(args))],
        out_specs=[in_vmem] * len(outs),
        scratch_shapes=list(scratch),
        compiler_params=pltpu.CompilerParams(vmem_limit_bytes=vmem * 1024 * 1024),
        cost_estimate=pl.CostEstimate(
            flops=weight << 20, bytes_accessed=weight << 20, transcendentals=0
        ),
    )(*args)


def at_slots(values, table, b):
    cap, interface = table.shape[1] // BLOCKS, values.shape[1]
    slot = lax.broadcasted_iota(jnp.int32, (interface, cap), 0).astype(F32)
    named = slot == table[:, b * cap : (b + 1) * cap]
    return dot_nn(values, jnp.where(named, 1.0, 0.0).astype(BF16))


def from_slots(values, table, b):
    return at_slots(values, table, b).astype(BF16)


def to_slots(blocks, columns_ref, interface):
    slot = lax.broadcasted_iota(jnp.int32, (columns_ref.shape[0], interface), 1).astype(F32)
    total = None
    for block, b in zip(blocks, RECEIVE_ORDER):
        named = slot == columns_ref[:, b : b + 1]
        part = dot_nn(block, jnp.where(named, 1.0, 0.0).astype(BF16))
        total = part if total is None else total + part
    return total


def first_exchange_body(rows_ref, fields_ref, columns_ref, *block_refs):
    cases, cap = block_refs[0].shape
    table = rows_ref[TABLE : TABLE + 1]
    for b in range(BLOCKS):
        block_refs[b][...] = from_slots(fields_ref[:cases], table, b)
    lane = lax.broadcasted_iota(jnp.int32, columns_ref.shape, 1)
    columns = jnp.zeros(columns_ref.shape, F32)
    for b in range(BLOCKS):
        column = row_to_column(table[:, b * cap : (b + 1) * cap])
        columns = jnp.where(lane == b, column, columns)
    columns_ref[...] = columns


def load_factor(factor_ref, held_ref, semaphores):
    size = held_ref.shape[0] // PIECES
    copies = []
    for i in range(PIECES):
        piece = pl.ds(size * i, size)
        copies.append(
            pltpu.make_async_copy(factor_ref.at[piece], held_ref.at[piece], semaphores.at[i])
        )
        copies[i].start()
    return copies


def times_factor(operand, held_ref, copies):
    size = held_ref.shape[0] // PIECES
    total = None
    for i in range(PIECES):
        copies[i].wait()
        part = dot_nn(operand[:, size * i : size * i + size], held_ref[size * i : size * i + size])
        total = part if total is None else total + part
    return total


def dirichlet_body(*refs):
    columns_ref, rows_ref, fields_ref, factor_ref = refs[BLOCKS : BLOCKS + 4]
    residual_ref, out_ref, live_ref, rho_ref, *block_refs = refs[BLOCKS + 4 : -2]
    held_ref, semaphores = refs[-2:]
    copies = load_factor(factor_ref, held_ref, semaphores)
    cases, interface = residual_ref.shape
    ones = jnp.ones((16, block_refs[0].shape[1]), BF16)
    blocks = [jnp.concatenate([ref[...], ones], axis=0) for ref in refs[:BLOCKS]]
    spread = to_slots(blocks, columns_ref, interface)
    live = spread[cases : cases + 8]
    residual = live[0:1] * (fields_ref[:cases].astype(F32) - spread[:cases])
    middle = times_factor(residual.astype(BF16), held_ref, copies).astype(BF16)
    diag = rows_ref[DIR_DIAG : DIR_DIAG + 1]
    out = (0.5 * (diag * residual + dot_nt(middle, held_ref[...]))).astype(BF16)
    table = rows_ref[TABLE : TABLE + 1]
    for b in range(BLOCKS):
        block_refs[b][...] = from_slots(out, table, b)
    live_ref[...] = live
    residual_ref[...] = residual
    out_ref[...] = out
    rho = column_to_row(jnp.sum(residual * out.astype(F32), axis=1, keepdims=True))
    rho_ref[...] = jnp.broadcast_to(rho, rho_ref.shape)


def schur_first_body(*refs):
    maps_ref, mine_ref, index_ref, dealt_ref, send_ref = refs[BLOCKS:]
    cap = refs[0].shape[1]
    corner_in = mine_ref[...]
    for ref, b in zip(refs[:BLOCKS], RECEIVE_ORDER):
        corner_in = corner_in - dot_nt(maps_ref[:24, b * cap : (b + 1) * cap], ref[...])
    corner_in = 0.5 * corner_in
    groups = [corner_in[0:8], corner_in[8:16], corner_in[16:24], index_lanes(index_ref[...])]
    tile = jnp.concatenate(groups, axis=1).astype(BF16)
    count, depth, _ = send_ref.shape
    send_ref[:, :, :LANES] = jnp.broadcast_to(tile[None], (count, depth, LANES))
    send_ref[:, :, LANES:] = dealt_ref[...]


def schur_second_body(*refs):
    out_ref, live_ref, columns_ref, rho_ref, rows_ref, factor_ref = refs[BLOCKS : BLOCKS + 6]
    direction_ref, local_ref, sent_ref, scalars_ref, held_ref, semaphores = refs[BLOCKS + 6 :]
    copies = load_factor(factor_ref, held_ref, semaphores)
    received = to_slots([ref[...] for ref in refs[:BLOCKS]], columns_ref, out_ref.shape[1])
    direction = 0.5 * (live_ref[0:1] * (out_ref[...].astype(F32) - received))
    direction_ref[...] = direction
    wide = times_factor(direction.astype(BF16), held_ref, copies)
    middle = wide.astype(BF16)
    scaled = rows_ref[SCHUR_DIAG : SCHUR_DIAG + 1] * direction
    local = scaled + dot_nt(middle, held_ref[...])
    local_ref[...] = local
    cases, interface = local.shape
    values = jnp.concatenate([part.astype(BF16) for part in three_parts(local)], axis=0)
    cap = interface // BLOCKS
    for b in range(BLOCKS):
        picked = at_slots(values, rows_ref[TABLE : TABLE + 1], b)
        exact = (picked[:cases] + picked[cases : 2 * cases]) + picked[2 * cases :]
        sent_ref[:, b * cap : (b + 1) * cap] = exact
    curve = jnp.sum(scaled * direction, axis=1, keepdims=True)
    curve = curve + jnp.sum(wide * middle.astype(F32), axis=1, keepdims=True)
    scalars = [rho_ref[0:1], column_to_row(curve), jnp.zeros((6, curve.shape[0]), F32)]
    scalars = jnp.concatenate(scalars, axis=0)
    scalars_ref[...] = jnp.concatenate([scalars, jnp.zeros((8, 96), F32)], axis=1)


def index_lanes(corner_row):
    corners = corner_row.shape[1]
    row = lax.broadcasted_iota(jnp.int32, (8, corners), 0)
    lane = lax.broadcasted_iota(jnp.int32, (8, corners), 1)
    place = lax.broadcasted_iota(jnp.int32, (8, 32), 1)
    tile = jnp.zeros((8, 32), F32)
    for q in range(3):
        mine = jnp.where(lane == 8 * q + row, corner_row, 0.0)
        value = jnp.sum(mine, axis=1, keepdims=True).astype(jnp.int32)
        tile = jnp.where(place == 2 * q, (value // 8).astype(F32), tile)
        tile = jnp.where(place == 2 * q + 1, (value % 8).astype(F32), tile)
    return tile


def deal_columns_body(*refs):
    out_ref, live_ref, rows_ref, fields_ref, send_ref, maps_ref, mine_ref = refs[4:]
    cases, cap = out_ref.shape[0], rows_ref.shape[1] // BLOCKS
    for b in range(BLOCKS):
        picked = at_slots(fields_ref[cases:], rows_ref[TABLE : TABLE + 1], b)
        maps_ref[:, b * cap : (b + 1) * cap] = picked.astype(BF16)
    shared = (live_ref[0:1] * out_ref[...].astype(F32)).astype(BF16)
    mine_ref[...] = dot_nt(fields_ref[cases : cases + 24], shared)
    rows = [ref[...].astype(F32) for ref in refs[:4]]
    depth, lanes = rows[0].shape
    group = lax.broadcasted_iota(jnp.int32, (depth, lanes), 1) // 32 % 4
    for t in range(4):
        dealt = jnp.zeros((depth, lanes), F32)
        for a in range(4):
            shift = (32 * (a - t)) % lanes
            moved = pltpu.roll(rows[a], shift, 1) if shift else rows[a]
            dealt = jnp.where(group == a, moved, dealt)
        for quad in range(lanes // LANES):
            tile = dealt[:, quad * LANES : (quad + 1) * LANES]
            send_ref[4 * quad + t] = tile.astype(BF16)


def coarse_first_body(sent_ref, scalars_ref, picked_ref, send_ref):
    count, depth, _ = sent_ref.shape
    size = count * depth
    sent = sent_ref[...].astype(F32)
    corner = sent[:, :, :LANES].reshape(size, LANES)
    columns = sent[:, :, LANES:].reshape(size, LANES).astype(BF16)
    place = lax.broadcasted_iota(jnp.int32, (size, size), 1).astype(F32)
    lane_group = (lax.broadcasted_iota(jnp.int32, (size, LANES), 1) // 32).astype(F32)
    near = lax.broadcasted_iota(jnp.int32, (LANES, LANES), 0)
    far = lax.broadcasted_iota(jnp.int32, (LANES, LANES), 1)
    total = jnp.zeros((size, LANES), F32)
    for q in range(3):
        upper, lower = corner[:, 96 + 2 * q : 97 + 2 * q], corner[:, 97 + 2 * q : 98 + 2 * q]
        member = jnp.floor(upper * 0.25)
        onehot = jnp.where(place == member * 8.0 + lower, 1.0, 0.0).astype(BF16)
        rows = dot_nn(onehot, columns)
        rows = jnp.where(lane_group == upper - 4.0 * member, rows, 0.0).astype(BF16)
        fold = jnp.where((near % 32 == far % 32) & (far // 32 == q), 1.0, 0.0).astype(BF16)
        total = total + dot_nn(rows, fold)
    picked = total.astype(BF16)
    picked_ref[...] = picked
    products = dot_tn(picked, corner.astype(BF16))
    middle = products[:32, :32]
    for q in range(1, 3):
        middle = middle + products[32 * q : 32 * q + 32, 32 * q : 32 * q + 32]
    send_ref[...] = jnp.concatenate([fold_rows(middle), scalars_ref[...]], axis=0)


def coarse_second_body(own_ref, one_ref, two_ref, three_ref, picked_ref, send_ref):
    total = (own_ref[...] + two_ref[...]) + (one_ref[...] + three_ref[...])
    middle = unfold_rows(total[:8])
    rounded = middle.astype(BF16)
    square = jnp.sum(middle * rounded.astype(F32), axis=0, keepdims=True)
    wide = jnp.concatenate([middle] * 4, axis=1)
    wide = jnp.concatenate([wide] * 4, axis=0)
    near = lax.broadcasted_iota(jnp.int32, wide.shape, 0) // 32
    far = lax.broadcasted_iota(jnp.int32, wide.shape, 1) // 32
    diagonal = jnp.where(near == far, wide, 0.0).astype(BF16)
    out = dot_nn(picked_ref[...], diagonal)
    rho, curve = total[8:9, :32], total[9:10, :32] + square
    zero = jnp.zeros((2, 32), F32)
    scalars = jnp.concatenate(three_parts(rho) + three_parts(curve) + [zero], axis=0)
    extra = jnp.concatenate([jnp.zeros((8, 96), F32), scalars], axis=1)
    send_ref[...] = (out.reshape(send_ref.shape) + extra[None]).astype(BF16)


def schur_last_body(coarse_ref, local_ref, fields_ref, sent_ref, maps_ref, *out_refs):
    schur_ref, step_ref, *block_refs = out_refs
    cases = local_ref.shape[0]
    rows = unfold_rows(jnp.sum(coarse_ref[...].astype(F32), axis=0))
    picked = rows[:24].astype(BF16)
    cap = block_refs[0].shape[1]
    blocks = (sent_ref[...] + dot_tn(picked, maps_ref[:24])).astype(BF16)
    for b in range(BLOCKS):
        block_refs[b][...] = blocks[:, b * cap : (b + 1) * cap]
    schur = local_ref[...] + dot_tn(picked, fields_ref[cases : cases + 24])
    schur_ref[...] = schur.astype(BF16)
    rho = jnp.sum(rows[24:27], axis=0, keepdims=True)
    curve = 2.0 * jnp.sum(rows[27:30], axis=0, keepdims=True)
    step_ref[...] = jnp.broadcast_to(row_to_column(rho / curve), step_ref.shape)


def update_body(*refs):
    schur_ref, step_ref, live_ref, direction_ref, residual_ref, columns_ref = refs[
        BLOCKS : BLOCKS + 6
    ]
    multipliers_ref, new_residual_ref = refs[BLOCKS + 6 :]
    multipliers_ref[...] = step_ref[:, 0:1] * direction_ref[...]
    received = to_slots([ref[...] for ref in refs[:BLOCKS]], columns_ref, schur_ref.shape[1])
    image = live_ref[0:1] * (schur_ref[...].astype(F32) - received)
    new_residual_ref[...] = residual_ref[...] - step_ref[:, 0:1] * image


def exchange(blocks):
    count = lax.axis_size("sub")
    received = [None] * BLOCKS
    for b in range(BLOCKS):
        route = [(i, (i + OFFSETS[b]) % count) for i in range(count)]
        received[(b + 3) % BLOCKS] = lax.ppermute(blocks[b], "sub", route)
    return [received[b] for b in RECEIVE_ORDER]


def to_groups(block):
    count = lax.axis_size("grp")
    return [
        lax.ppermute(block, "grp", [(i, (i + k) % count) for i in range(count)])
        for k in range(1, count)
    ]


def on_device(
    load_source,
    schur_diag,
    schur_factor,
    dir_diag,
    dir_factor,
    corner_map,
    corner_row,
    coarse_factor,
    slot_table,
):
    source = load_source[0, 0]
    schur_factor = schur_factor[0, 0]
    dir_factor = dir_factor[0, 0]
    cases, interface = source.shape
    subs, groups = lax.axis_size("sub"), lax.axis_size("grp")
    table = slot_table.reshape(1, -1)
    total = table.shape[1]
    cap = total // BLOCKS
    field = (cases, interface)
    depth, coarse_size = coarse_factor.shape

    def blocks_of(rows):
        return [((rows, cap), BF16)] * BLOCKS

    coarse_rows = [coarse_factor] + to_groups(coarse_factor)
    rows = jnp.concatenate([table.astype(F32), dir_diag[0], schur_diag[0]], axis=0)
    fields = jnp.concatenate([source, corner_map[0, 0]], axis=0)
    fields = jnp.pad(fields, ((0, -fields.shape[0] % 16), (0, 0)))
    columns, *blocks = call(
        first_exchange_body, [((cap, LANES), F32)] + blocks_of(cases), 4, rows, fields
    )
    factor_scratch = [pltpu.VMEM((interface, interface), BF16), pltpu.SemaphoreType.DMA((PIECES,))]
    firsts = exchange(blocks)
    residual, dir_out, live, rho, *blocks = call(
        dirichlet_body,
        [(field, F32), (field, BF16), ((8, interface), F32), ((8, cases), F32)] + blocks_of(cases),
        16,
        *firsts,
        columns,
        rows,
        fields,
        dir_factor,
        scratch=factor_scratch,
        in_hbm=(BLOCKS + 3,),
        vmem=50,
    )
    seconds = exchange(blocks)
    *coarse_rows, corner, rho = lax.optimization_barrier((*coarse_rows, corner_row[0], rho))
    away = (lax.axis_index("grp") - corner // 8 % 4) % groups
    corner = ((corner // 32 * 4 + away) * 8 + corner % 8).astype(F32)
    corner = jnp.pad(corner, ((0, 0), (0, LANES - corner.shape[1])))
    spare = fields.shape[0] - cases
    dealt, maps, mine = call(
        deal_columns_body,
        [((subs, depth, LANES), BF16), ((spare, total), BF16), ((24, cases), F32)],
        2,
        *coarse_rows,
        dir_out,
        live,
        rows,
        fields,
    )
    (corner_in,) = call(
        schur_first_body,
        [((subs, depth, 2 * LANES), BF16)],
        4,
        *seconds,
        maps,
        mine,
        corner,
        dealt,
    )
    corner_in = lax.all_to_all(corner_in, "sub", 0, 0, tiled=True)
    direction, local, sent, scalars = call(
        schur_second_body,
        [(field, F32), (field, F32), (field, F32), ((8, LANES), F32)],
        8,
        *seconds,
        dir_out,
        live,
        columns,
        rho,
        rows,
        schur_factor,
        scratch=factor_scratch,
        in_hbm=(BLOCKS + 5,),
        vmem=50,
    )
    picked, parts = call(
        coarse_first_body,
        [((subs * depth, LANES), BF16), ((16, LANES), F32)],
        4,
        corner_in,
        scalars,
    )
    local, parts = lax.optimization_barrier((local, parts))
    (coarse,) = call(
        coarse_second_body,
        [((subs, 8, LANES), BF16)],
        2,
        parts,
        *to_groups(parts),
        picked,
    )
    coarse = lax.all_to_all(coarse, "sub", 0, 0, tiled=True)
    schur_out, step, *blocks = call(
        schur_last_body,
        [(field, BF16), ((cases, LANES), F32)] + blocks_of(cases),
        8,
        coarse,
        local,
        fields,
        sent,
        maps,
    )
    multipliers, residual = call(
        update_body,
        [(field, F32), (field, F32)],
        8,
        *exchange(blocks),
        schur_out,
        step,
        live,
        direction,
        residual,
        columns,
    )
    return (multipliers[None, None], residual[None, None])


def solution(mesh):
    return jax.shard_map(
        on_device,
        mesh=mesh,
        in_specs=(
            P("grp", "sub", None, None),
            P("grp", "sub", None),
            P("grp", "sub", None, None),
            P("grp", "sub", None),
            P("grp", "sub", None, None),
            P("grp", "sub", None, None),
            P("grp", "sub", None),
            P(("sub", "grp"), None),
            P("grp", "sub", None, None),
        ),
        out_specs=(P("grp", "sub", None, None), P("grp", "sub", None, None)),
        check_vma=False,
    )
```

```python
import jax
import jax.numpy as jnp
from jax import lax
from jax.experimental import pallas as pl
from jax.experimental.pallas import tpu as pltpu
from jax.sharding import PartitionSpec as P

OFFSETS = (1, 2, 5, -1, -2, -5)
BLOCKS = len(OFFSETS)
F32 = jnp.float32
BF16 = jnp.bfloat16
LANES = 128
PIECES = 6
RECEIVE_ORDER = (2, 1, 0, 5, 4, 3)
TABLE, DIR_DIAG, SCHUR_DIAG = 0, 1, 2


def dot_nn(a, b):
    return jnp.dot(a, b, preferred_element_type=F32)


def dot_nt(a, b):
    return lax.dot_general(a, b, (((1,), (1,)), ((), ())), preferred_element_type=F32)


def dot_tn(a, b):
    return lax.dot_general(a, b, (((0,), (0,)), ((), ())), preferred_element_type=F32)


def column_to_row(column):
    n = column.shape[0]
    same = lax.broadcasted_iota(jnp.int32, (n, n), 0) == lax.broadcasted_iota(jnp.int32, (n, n), 1)
    return jnp.sum(jnp.where(same, column, 0.0), axis=0, keepdims=True)


def row_to_column(row):
    n = row.shape[1]
    same = lax.broadcasted_iota(jnp.int32, (n, n), 0) == lax.broadcasted_iota(jnp.int32, (n, n), 1)
    return jnp.sum(jnp.where(same, row, 0.0), axis=1, keepdims=True)


def three_parts(value):
    first = value.astype(BF16).astype(F32)
    rest = value - first
    second = rest.astype(BF16).astype(F32)
    third = (rest - second).astype(BF16).astype(F32)
    return [first, second, third]


def fold_rows(rows):
    n = rows.shape[0] // 4
    return jnp.concatenate([rows[n * i : n * i + n] for i in range(4)], axis=1)


def unfold_rows(tile):
    n = tile.shape[1] // 4
    return jnp.concatenate([tile[:, n * i : n * i + n] for i in range(4)], axis=0)


def call(body, outs, weight, *args, scratch=(), in_hbm=(), vmem=20):
    in_vmem = pl.BlockSpec(memory_space=pltpu.VMEM)
    left = pl.BlockSpec(memory_space=pltpu.HBM)
    return pl.pallas_call(
        body,
        out_shape=[jax.ShapeDtypeStruct(shape, dtype) for shape, dtype in outs],
        in_specs=[left if i in in_hbm else in_vmem for i in range(len(args))],
        out_specs=[in_vmem] * len(outs),
        scratch_shapes=list(scratch),
        compiler_params=pltpu.CompilerParams(vmem_limit_bytes=vmem * 1024 * 1024),
        cost_estimate=pl.CostEstimate(
            flops=weight << 20, bytes_accessed=weight << 20, transcendentals=0
        ),
    )(*args)


def at_slots(values, table, b):
    cap, interface = table.shape[1] // BLOCKS, values.shape[1]
    slot = lax.broadcasted_iota(jnp.int32, (interface, cap), 0).astype(F32)
    named = slot == table[:, b * cap : (b + 1) * cap]
    return dot_nn(values, jnp.where(named, 1.0, 0.0).astype(BF16))


def from_slots(values, table, b):
    return at_slots(values, table, b).astype(BF16)


def to_slots(blocks, columns_ref, interface):
    slot = lax.broadcasted_iota(jnp.int32, (columns_ref.shape[0], interface), 1).astype(F32)
    total = None
    for block, b in zip(blocks, RECEIVE_ORDER):
        named = slot == columns_ref[:, b : b + 1]
        part = dot_nn(block, jnp.where(named, 1.0, 0.0).astype(BF16))
        total = part if total is None else total + part
    return total


def first_exchange_body(rows_ref, fields_ref, columns_ref, *block_refs):
    cases, cap = block_refs[0].shape
    table = rows_ref[TABLE : TABLE + 1]
    for b in range(BLOCKS):
        block_refs[b][...] = from_slots(fields_ref[:cases], table, b)
    lane = lax.broadcasted_iota(jnp.int32, columns_ref.shape, 1)
    columns = jnp.zeros(columns_ref.shape, F32)
    for b in range(BLOCKS):
        column = row_to_column(table[:, b * cap : (b + 1) * cap])
        columns = jnp.where(lane == b, column, columns)
    columns_ref[...] = columns


def load_factor(factor_ref, held_ref, semaphores):
    size = held_ref.shape[0] // PIECES
    copies = []
    for i in range(PIECES):
        piece = pl.ds(size * i, size)
        copies.append(
            pltpu.make_async_copy(factor_ref.at[piece], held_ref.at[piece], semaphores.at[i])
        )
        copies[i].start()
    return copies


def times_factor(operand, held_ref, copies):
    size = held_ref.shape[0] // PIECES
    total = None
    for i in range(PIECES):
        copies[i].wait()
        part = dot_nn(operand[:, size * i : size * i + size], held_ref[size * i : size * i + size])
        total = part if total is None else total + part
    return total


def dirichlet_body(*refs):
    columns_ref, rows_ref, fields_ref, factor_ref = refs[BLOCKS : BLOCKS + 4]
    residual_ref, out_ref, live_ref, rho_ref, *block_refs = refs[BLOCKS + 4 : -2]
    held_ref, semaphores = refs[-2:]
    copies = load_factor(factor_ref, held_ref, semaphores)
    cases, interface = residual_ref.shape
    ones = jnp.ones((16, block_refs[0].shape[1]), BF16)
    blocks = [jnp.concatenate([ref[...], ones], axis=0) for ref in refs[:BLOCKS]]
    spread = to_slots(blocks, columns_ref, interface)
    live = spread[cases : cases + 8]
    residual = live[0:1] * (fields_ref[:cases].astype(F32) - spread[:cases])
    middle = times_factor(residual.astype(BF16), held_ref, copies).astype(BF16)
    diag = rows_ref[DIR_DIAG : DIR_DIAG + 1]
    out = (0.5 * (diag * residual + dot_nt(middle, held_ref[...]))).astype(BF16)
    table = rows_ref[TABLE : TABLE + 1]
    for b in range(BLOCKS):
        block_refs[b][...] = from_slots(out, table, b)
    live_ref[...] = live
    residual_ref[...] = residual
    out_ref[...] = out
    rho = column_to_row(jnp.sum(residual * out.astype(F32), axis=1, keepdims=True))
    rho_ref[...] = jnp.broadcast_to(rho, rho_ref.shape)


def schur_first_body(*refs):
    maps_ref, mine_ref, index_ref, dealt_ref, send_ref = refs[BLOCKS:]
    cap = refs[0].shape[1]
    corner_in = mine_ref[...]
    for ref, b in zip(refs[:BLOCKS], RECEIVE_ORDER):
        corner_in = corner_in - dot_nt(maps_ref[:24, b * cap : (b + 1) * cap], ref[...])
    corner_in = 0.5 * corner_in
    corner = index_ref[...]
    away = (lax.axis_index("grp") + 4 - ((corner >> 3) & 3)) & 3
    corner = ((((corner >> 5) * 4 + away) * 8) + (corner & 7)).astype(F32)
    groups = [corner_in[0:8], corner_in[8:16], corner_in[16:24], index_lanes(corner)]
    tile = jnp.concatenate(groups, axis=1).astype(BF16)
    count, depth, _ = send_ref.shape
    send_ref[:, :, :LANES] = jnp.broadcast_to(tile[None], (count, depth, LANES))
    send_ref[:, :, LANES:] = dealt_ref[...]


def schur_second_body(*refs):
    out_ref, live_ref, columns_ref, rho_ref, rows_ref, factor_ref = refs[BLOCKS : BLOCKS + 6]
    direction_ref, local_ref, sent_ref, scalars_ref, held_ref, semaphores = refs[BLOCKS + 6 :]
    copies = load_factor(factor_ref, held_ref, semaphores)
    received = to_slots([ref[...] for ref in refs[:BLOCKS]], columns_ref, out_ref.shape[1])
    direction = 0.5 * (live_ref[0:1] * (out_ref[...].astype(F32) - received))
    direction_ref[...] = direction
    wide = times_factor(direction.astype(BF16), held_ref, copies)
    middle = wide.astype(BF16)
    scaled = rows_ref[SCHUR_DIAG : SCHUR_DIAG + 1] * direction
    local = scaled + dot_nt(middle, held_ref[...])
    local_ref[...] = local
    cases, interface = local.shape
    values = jnp.concatenate([part.astype(BF16) for part in three_parts(local)], axis=0)
    cap = interface // BLOCKS
    for b in range(BLOCKS):
        picked = at_slots(values, rows_ref[TABLE : TABLE + 1], b)
        exact = (picked[:cases] + picked[cases : 2 * cases]) + picked[2 * cases :]
        sent_ref[:, b * cap : (b + 1) * cap] = exact
    curve = jnp.sum(scaled * direction, axis=1, keepdims=True)
    curve = curve + jnp.sum(wide * middle.astype(F32), axis=1, keepdims=True)
    scalars = [rho_ref[0:1], column_to_row(curve), jnp.zeros((6, curve.shape[0]), F32)]
    scalars = jnp.concatenate(scalars, axis=0)
    scalars_ref[...] = jnp.concatenate([scalars, jnp.zeros((8, 96), F32)], axis=1)


def index_lanes(corner_row):
    corners = corner_row.shape[1]
    row = lax.broadcasted_iota(jnp.int32, (8, corners), 0)
    lane = lax.broadcasted_iota(jnp.int32, (8, corners), 1)
    place = lax.broadcasted_iota(jnp.int32, (8, 32), 1)
    tile = jnp.zeros((8, 32), F32)
    for q in range(3):
        mine = jnp.where(lane == 8 * q + row, corner_row, 0.0)
        value = jnp.sum(mine, axis=1, keepdims=True).astype(jnp.int32)
        tile = jnp.where(place == 2 * q, (value // 8).astype(F32), tile)
        tile = jnp.where(place == 2 * q + 1, (value % 8).astype(F32), tile)
    return tile


def deal_columns_body(*refs):
    out_ref, live_ref, rows_ref, fields_ref, send_ref, maps_ref, mine_ref = refs[4:]
    cases, cap = out_ref.shape[0], rows_ref.shape[1] // BLOCKS
    for b in range(BLOCKS):
        picked = at_slots(fields_ref[cases:], rows_ref[TABLE : TABLE + 1], b)
        maps_ref[:, b * cap : (b + 1) * cap] = picked.astype(BF16)
    shared = (live_ref[0:1] * out_ref[...].astype(F32)).astype(BF16)
    mine_ref[...] = dot_nt(fields_ref[cases : cases + 24], shared)
    rows = [ref[...].astype(F32) for ref in refs[:4]]
    depth, lanes = rows[0].shape
    group = lax.broadcasted_iota(jnp.int32, (depth, lanes), 1) // 32 % 4
    for t in range(4):
        dealt = jnp.zeros((depth, lanes), F32)
        for a in range(4):
            shift = (32 * (a - t)) % lanes
            moved = pltpu.roll(rows[a], shift, 1) if shift else rows[a]
            dealt = jnp.where(group == a, moved, dealt)
        for quad in range(lanes // LANES):
            tile = dealt[:, quad * LANES : (quad + 1) * LANES]
            send_ref[4 * quad + t] = tile.astype(BF16)


def coarse_first_body(sent_ref, scalars_ref, picked_ref, send_ref):
    count, depth, _ = sent_ref.shape
    size = count * depth
    sent = sent_ref[...].astype(F32)
    corner = sent[:, :, :LANES].reshape(size, LANES)
    columns = sent[:, :, LANES:].reshape(size, LANES).astype(BF16)
    place = lax.broadcasted_iota(jnp.int32, (size, size), 1).astype(F32)
    lane_group = (lax.broadcasted_iota(jnp.int32, (size, LANES), 1) // 32).astype(F32)
    near = lax.broadcasted_iota(jnp.int32, (LANES, LANES), 0)
    far = lax.broadcasted_iota(jnp.int32, (LANES, LANES), 1)
    total = jnp.zeros((size, LANES), F32)
    for q in range(3):
        upper, lower = corner[:, 96 + 2 * q : 97 + 2 * q], corner[:, 97 + 2 * q : 98 + 2 * q]
        member = jnp.floor(upper * 0.25)
        onehot = jnp.where(place == member * 8.0 + lower, 1.0, 0.0).astype(BF16)
        rows = dot_nn(onehot, columns)
        rows = jnp.where(lane_group == upper - 4.0 * member, rows, 0.0).astype(BF16)
        fold = jnp.where((near % 32 == far % 32) & (far // 32 == q), 1.0, 0.0).astype(BF16)
        total = total + dot_nn(rows, fold)
    picked = total.astype(BF16)
    picked_ref[...] = picked
    products = dot_tn(picked, corner.astype(BF16))
    middle = products[:32, :32]
    for q in range(1, 3):
        middle = middle + products[32 * q : 32 * q + 32, 32 * q : 32 * q + 32]
    send_ref[...] = jnp.concatenate([fold_rows(middle), scalars_ref[...]], axis=0)


def coarse_second_body(own_ref, one_ref, two_ref, three_ref, picked_ref, send_ref):
    total = (own_ref[...] + two_ref[...]) + (one_ref[...] + three_ref[...])
    middle = unfold_rows(total[:8])
    rounded = middle.astype(BF16)
    square = jnp.sum(middle * rounded.astype(F32), axis=0, keepdims=True)
    wide = jnp.concatenate([middle] * 4, axis=1)
    wide = jnp.concatenate([wide] * 4, axis=0)
    near = lax.broadcasted_iota(jnp.int32, wide.shape, 0) // 32
    far = lax.broadcasted_iota(jnp.int32, wide.shape, 1) // 32
    diagonal = jnp.where(near == far, wide, 0.0).astype(BF16)
    out = dot_nn(picked_ref[...], diagonal)
    rho, curve = total[8:9, :32], total[9:10, :32] + square
    zero = jnp.zeros((2, 32), F32)
    scalars = jnp.concatenate(three_parts(rho) + three_parts(curve) + [zero], axis=0)
    extra = jnp.concatenate([jnp.zeros((8, 96), F32), scalars], axis=1)
    send_ref[...] = (out.reshape(send_ref.shape) + extra[None]).astype(BF16)


def schur_last_body(coarse_ref, local_ref, fields_ref, sent_ref, maps_ref, *out_refs):
    schur_ref, step_ref, *block_refs = out_refs
    cases = local_ref.shape[0]
    rows = unfold_rows(jnp.sum(coarse_ref[...].astype(F32), axis=0))
    picked = rows[:24].astype(BF16)
    cap = block_refs[0].shape[1]
    blocks = (sent_ref[...] + dot_tn(picked, maps_ref[:24])).astype(BF16)
    for b in range(BLOCKS):
        block_refs[b][...] = blocks[:, b * cap : (b + 1) * cap]
    schur = local_ref[...] + dot_tn(picked, fields_ref[cases : cases + 24])
    schur_ref[...] = schur.astype(BF16)
    rho = jnp.sum(rows[24:27], axis=0, keepdims=True)
    curve = 2.0 * jnp.sum(rows[27:30], axis=0, keepdims=True)
    step_ref[...] = jnp.broadcast_to(row_to_column(rho / curve), step_ref.shape)


def update_body(*refs):
    schur_ref, step_ref, live_ref, direction_ref, residual_ref, columns_ref = refs[
        BLOCKS : BLOCKS + 6
    ]
    multipliers_ref, new_residual_ref = refs[BLOCKS + 6 :]
    multipliers_ref[...] = step_ref[:, 0:1] * direction_ref[...]
    received = to_slots([ref[...] for ref in refs[:BLOCKS]], columns_ref, schur_ref.shape[1])
    image = live_ref[0:1] * (schur_ref[...].astype(F32) - received)
    new_residual_ref[...] = residual_ref[...] - step_ref[:, 0:1] * image


def exchange(blocks):
    count = lax.axis_size("sub")
    received = [None] * BLOCKS
    for b in range(BLOCKS):
        route = [(i, (i + OFFSETS[b]) % count) for i in range(count)]
        received[(b + 3) % BLOCKS] = lax.ppermute(blocks[b], "sub", route)
    return [received[b] for b in RECEIVE_ORDER]


def to_groups(block):
    count = lax.axis_size("grp")
    return [
        lax.ppermute(block, "grp", [(i, (i + k) % count) for i in range(count)])
        for k in range(1, count)
    ]


def on_device(
    load_source,
    schur_diag,
    schur_factor,
    dir_diag,
    dir_factor,
    corner_map,
    corner_row,
    coarse_factor,
    slot_table,
):
    source = load_source[0, 0]
    schur_factor = schur_factor[0, 0]
    dir_factor = dir_factor[0, 0]
    cases, interface = source.shape
    subs, groups = lax.axis_size("sub"), lax.axis_size("grp")
    table = slot_table.reshape(1, -1)
    total = table.shape[1]
    cap = total // BLOCKS
    field = (cases, interface)
    depth, coarse_size = coarse_factor.shape

    def blocks_of(rows):
        return [((rows, cap), BF16)] * BLOCKS

    coarse_rows = [coarse_factor] + to_groups(coarse_factor)
    rows = jnp.concatenate([table.astype(F32), dir_diag[0], schur_diag[0]], axis=0)
    fields = jnp.concatenate([source, corner_map[0, 0]], axis=0)
    fields = jnp.pad(fields, ((0, -fields.shape[0] % 16), (0, 0)))
    columns, *blocks = call(
        first_exchange_body, [((cap, LANES), F32)] + blocks_of(cases), 4, rows, fields
    )
    factor_scratch = [pltpu.VMEM((interface, interface), BF16), pltpu.SemaphoreType.DMA((PIECES,))]
    firsts = exchange(blocks)
    residual, dir_out, live, rho, *blocks = call(
        dirichlet_body,
        [(field, F32), (field, BF16), ((8, interface), F32), ((8, cases), F32)] + blocks_of(cases),
        16,
        *firsts,
        columns,
        rows,
        fields,
        dir_factor,
        scratch=factor_scratch,
        in_hbm=(BLOCKS + 3,),
        vmem=50,
    )
    seconds = exchange(blocks)
    *coarse_rows, rho = lax.optimization_barrier((*coarse_rows, rho))
    spare = fields.shape[0] - cases
    dealt, maps, mine = call(
        deal_columns_body,
        [((subs, depth, LANES), BF16), ((spare, total), BF16), ((24, cases), F32)],
        2,
        *coarse_rows,
        dir_out,
        live,
        rows,
        fields,
    )
    (corner_in,) = call(
        schur_first_body,
        [((subs, depth, 2 * LANES), BF16)],
        4,
        *seconds,
        maps,
        mine,
        corner_row[0],
        dealt,
    )
    corner_in = lax.all_to_all(corner_in, "sub", 0, 0, tiled=True)
    direction, local, sent, scalars = call(
        schur_second_body,
        [(field, F32), (field, F32), (field, F32), ((8, LANES), F32)],
        8,
        *seconds,
        dir_out,
        live,
        columns,
        rho,
        rows,
        schur_factor,
        scratch=factor_scratch,
        in_hbm=(BLOCKS + 5,),
        vmem=50,
    )
    picked, parts = call(
        coarse_first_body,
        [((subs * depth, LANES), BF16), ((16, LANES), F32)],
        4,
        corner_in,
        scalars,
    )
    local, parts = lax.optimization_barrier((local, parts))
    (coarse,) = call(
        coarse_second_body,
        [((subs, 8, LANES), BF16)],
        2,
        parts,
        *to_groups(parts),
        picked,
    )
    coarse = lax.all_to_all(coarse, "sub", 0, 0, tiled=True)
    schur_out, step, *blocks = call(
        schur_last_body,
        [(field, BF16), ((cases, LANES), F32)] + blocks_of(cases),
        8,
        coarse,
        local,
        fields,
        sent,
        maps,
    )
    multipliers, residual = call(
        update_body,
        [(field, F32), (field, F32)],
        8,
        *exchange(blocks),
        schur_out,
        step,
        live,
        direction,
        residual,
        columns,
    )
    return (multipliers[None, None], residual[None, None])


def solution(mesh):
    return jax.shard_map(
        on_device,
        mesh=mesh,
        in_specs=(
            P("grp", "sub", None, None),
            P("grp", "sub", None),
            P("grp", "sub", None, None),
            P("grp", "sub", None),
            P("grp", "sub", None, None),
            P("grp", "sub", None, None),
            P("grp", "sub", None),
            P(("sub", "grp"), None),
            P("grp", "sub", None, None),
        ),
        out_specs=(P("grp", "sub", None, None), P("grp", "sub", None, None)),
        check_vma=False,
    )
```
